128 devices in a mesh: beam: 16 (over x_lo, y, core), seg: 8 (over z, x_hi).
Axes of the slice: x: 4 (x_hi: 2, x_lo: 2; x = x_hi * 2 + x_lo), y: 4, z: 4, core: 2. Of those that a mesh axis runs over, the one named last changes fastest.
Arguments:
- voltages: bfloat16 [2, 256, 8, 65536], P(None, 'beam', 'seg'), may hold values from -6 to 6
- surv_taps: bfloat16 [32], replicated, may hold values from -1 to 1
- ref_taps: bfloat16 [32], replicated, may hold values from -1 to 1
- tx_owner: int32 [4], replicated, may hold values from 0 to 255
- delay_start: int32 [4], replicated, may hold values from 0 to 384
- doppler_start: int32 [4], replicated, may hold values from 0 to 128
Outputs:
- maps: float32 [4, 256, 128, 128], P(None, 'beam', 'seg')
The draws below stay inside these ranges and needn't reach their ends.
All inputs are finite; a program needn't handle non-finite values.
Results may differ from the reference program's by a relative error of at most 0.0027.
Values may be sent and summed in bfloat16 or wider, within the bound.
A program may use at most 128 MiB of HBM per device.

```python
import jax
import jax.numpy as jnp
from jax import lax

SEG_DEV = 1
TX = 4
DECIM = 4
TAPS = 32
BLOCK_LEN = 64
BLOCKS = 256
DELAYS = 128
DOPPLER = 128
MAXDELAY = 512
RAW = 65536
BEAMS = 256
SEGMENTS = 8
N_SEG = 8


def with_ends(drawn, rng, smallest, high):
    extent = drawn.shape
    spot = [jax.random.randint(jax.random.fold_in(rng, axis), (), 0, extent[axis]) for axis in range(len(extent))]
    drawn = drawn.at[tuple(spot)].set(smallest)
    longest = extent.index(max(extent))
    spot[longest] = (spot[longest] + 1) % extent[longest]
    return drawn.at[tuple(spot)].set(high)


def level_of(rng, dims, split, low, largest):
    loudness = 1.0
    for dim, shards_of in split:
        heights = jax.random.uniform(jax.random.fold_in(jax.random.fold_in(rng, 6), dim), (shards_of,), jnp.float32, low / len(split), largest / len(split))
        loudness = loudness * jnp.repeat(jnp.exp(heights), dims[dim] // shards_of).reshape((-1,) + (1,) * (len(dims) - 1 - dim))
    return loudness


def centred(own_key, shape, deviation, reach, pieces=(), held_as=jnp.bfloat16):
    result = deviation * jax.random.normal(own_key, shape, jnp.float32)
    if pieces:
        result = result * level_of(own_key, shape, pieces, -0.22, 0.18)
    return jnp.clip(result, -reach, reach).astype(held_as)


def setup_inputs(seed: int = 0) -> dict:
    streams_of = jax.random.split(jax.random.key(seed), 7)
    voltages = centred(streams_of[0], (2, BEAMS, SEGMENTS, RAW), 1.0, 6.0, ((1, 16), (2, 8)))
    surv_taps = centred(streams_of[1], (TAPS,), TAPS ** -0.5, 1.0)
    ref_taps = centred(streams_of[2], (TAPS,), TAPS ** -0.5, 1.0)
    tx_owner = with_ends(jax.random.randint(streams_of[3], (TX,), 0, BEAMS), jax.random.fold_in(streams_of[3], 1), 0, BEAMS - 1).astype(jnp.int32)
    delay_start = with_ends(jax.random.randint(streams_of[4], (TX,), 0, MAXDELAY - DELAYS + 1), jax.random.fold_in(streams_of[4], 1), 0, MAXDELAY - DELAYS).astype(jnp.int32)
    doppler_start = with_ends(jax.random.randint(streams_of[5], (TX,), 0, BLOCKS - DOPPLER + 1), jax.random.fold_in(streams_of[5], 1), 0, BLOCKS - DOPPLER).astype(jnp.int32)
    return dict(voltages=voltages, surv_taps=surv_taps, ref_taps=ref_taps, tx_owner=tx_owner, delay_start=delay_start, doppler_start=doppler_start)


def decimate(raw, taps):
    count = raw.shape[-1] // DECIM
    pads = [(0, 0)] * (raw.ndim - 1) + [(TAPS - 1, 0)]
    padded = jnp.pad(raw, pads)
    total = jnp.zeros(raw.shape[:-1] + (count,), jnp.float32)
    for tap in range(TAPS):
        begin = TAPS - 1 - tap
        piece = padded[..., begin:begin + DECIM * count:DECIM]
        total = total + taps[tap].astype(jnp.float32) * piece.astype(jnp.float32)
    return total.astype(jnp.bfloat16)


def segment_power(surv_seg, ref_seg, d_lo, cos_t, sin_t):
    beams = surv_seg.shape[1]
    span = BLOCK_LEN + DELAYS - 1
    extra = (DELAYS - 1 + BLOCK_LEN - 1) // BLOCK_LEN
    blocks_s = surv_seg.reshape(2, beams, BLOCKS, BLOCK_LEN).astype(jnp.float32)
    rpad = jnp.pad(ref_seg, ((0, 0), (MAXDELAY, extra * BLOCK_LEN)))
    start = (MAXDELAY - (DELAYS - 1) - d_lo).astype(jnp.int32)
    rwin = lax.dynamic_slice_in_dim(rpad, start, (BLOCKS + extra) * BLOCK_LEN, 1)
    rwin = rwin.reshape(2, BLOCKS + extra, BLOCK_LEN)
    window = jnp.concatenate([rwin[:, e:e + BLOCKS] for e in range(extra + 1)], axis=2)[..., :span]
    tiled = jnp.tile(window, (1, 1, BLOCK_LEN + 1))[..., :BLOCK_LEN * (span + 1)]
    toeplitz = tiled.reshape(2, BLOCKS, BLOCK_LEN, span + 1)[..., :DELAYS].astype(jnp.float32)
    scale = BLOCK_LEN ** -0.5
    s_re, s_im = blocks_s[0], blocks_s[1]
    u_re, u_im = toeplitz[0], toeplitz[1]
    c_re = (jnp.einsum("blm,lmi->bli", s_re, u_re) + jnp.einsum("blm,lmi->bli", s_im, u_im)) * scale
    c_im = (jnp.einsum("blm,lmi->bli", s_im, u_re) - jnp.einsum("blm,lmi->bli", s_re, u_im)) * scale
    c_re = c_re[..., ::-1].astype(jnp.bfloat16).astype(jnp.float32)
    c_im = c_im[..., ::-1].astype(jnp.bfloat16).astype(jnp.float32)
    cos_f = cos_t.astype(jnp.float32)
    sin_f = sin_t.astype(jnp.float32)
    x_re = jnp.einsum("blj,lf->bjf", c_re, cos_f) + jnp.einsum("blj,lf->bjf", c_im, sin_f)
    x_im = jnp.einsum("blj,lf->bjf", c_im, cos_f) - jnp.einsum("blj,lf->bjf", c_re, sin_f)
    return (x_re * x_re + x_im * x_im) * (1.0 / (4 * BLOCKS))


def tables(f_lo):
    ells = jnp.arange(BLOCKS, dtype=jnp.int32)
    freqs = f_lo.astype(jnp.int32) + jnp.arange(DOPPLER, dtype=jnp.int32) - BLOCKS // 2
    phase = (ells[:, None] * freqs[None, :]) % BLOCKS
    angle = (2.0 * jnp.pi / BLOCKS) * phase.astype(jnp.float32)
    return jnp.cos(angle).astype(jnp.bfloat16), jnp.sin(angle).astype(jnp.bfloat16)


def reference(voltages, surv_taps, ref_taps, tx_owner, delay_start, doppler_start):
    surv = decimate(voltages, surv_taps)

    def slot_map(trans):
        raw_ref = lax.dynamic_index_in_dim(voltages, tx_owner[trans].astype(jnp.int32), 1, keepdims=False)
        ref = decimate(raw_ref, ref_taps)
        d_lo = delay_start[trans]
        cos_t, sin_t = tables(doppler_start[trans])

        def group(total, index):
            for inner in range(SEG_DEV):
                seg = (index * SEG_DEV + inner).astype(jnp.int32)
                surv_seg = lax.dynamic_index_in_dim(surv, seg, 2, keepdims=False)
                ref_seg = lax.dynamic_index_in_dim(ref, seg, 1, keepdims=False)
                total = total + segment_power(surv_seg, ref_seg, d_lo, cos_t, sin_t)
            return total, None

        total, _ = lax.scan(group, jnp.zeros((BEAMS, DELAYS, DOPPLER), jnp.float32), jnp.arange(N_SEG, dtype=jnp.int32))
        return total / SEGMENTS

    return lax.map(slot_map, jnp.arange(TX, dtype=jnp.int32))
```

```python
import functools

import jax
import jax.numpy as jnp
import numpy as np
from jax import lax
from jax.experimental import pallas as pl
from jax.experimental.pallas import tpu as pltpu
from jax.sharding import PartitionSpec as P

TX = 4
DECIM = 4
TAPS = 32
BLOCK_LEN = 64
BLOCKS = 256
DELAYS = 128
DOPPLER = 128
LANES = 128
BEAMS_HERE = 16
WINDOWS = 128
WINDOWS_STEP = 16
STEPS = WINDOWS // WINDOWS_STEP
RAW_WINDOW = DECIM * LANES
BEAM = 16
SEG = 8
F32 = jnp.float32
BF16 = jnp.bfloat16
MESH = pl.DeviceIdType.MESH


def band_base(taps, backwards):
    rows = lax.broadcasted_iota(jnp.int32, (LANES, LANES), 0)
    cols = lax.broadcasted_iota(jnp.int32, (LANES, LANES), 1)
    if backwards:
        cols = LANES - 1 - cols
    offset = DECIM * cols - rows
    total = jnp.zeros((LANES, LANES), F32)
    for tap in range(TAPS):
        total = jnp.where(offset == tap, taps[tap], total)
    return total


def front_kernel(owner, delay, surv_taps, ref_taps, x, surv, ref, band, halo, picked):
    step = pl.program_id(0)
    me = lax.axis_index("beam")
    lane = lax.broadcasted_iota(jnp.int32, (LANES, LANES), 1)

    @pl.when(step == 0)
    def _():
        forward = band_base(surv_taps, False)
        backward = band_base(ref_taps, True)
        for part in range(5):
            shift = 32 * (part - 1)
            ahead = pltpu.roll(forward, shift % LANES, axis=1)
            behind = pltpu.roll(backward, -shift % LANES, axis=1)
            if part == 0:
                ahead = jnp.where(lane < 8, ahead, 0.0)
                behind = jnp.where(lane >= LANES - 8, behind, 0.0)
            else:
                ahead = jnp.where(lane >= shift, ahead, 0.0)
                behind = jnp.where(lane < LANES - shift, behind, 0.0)
            band[part * LANES : (part + 1) * LANES, :LANES] = ahead.astype(BF16)
            band[part * LANES : (part + 1) * LANES, LANES:] = behind.astype(BF16)
        halo[...] = jnp.zeros_like(halo)
        picked[WINDOWS * 32 :, :] = jnp.zeros((8 * 32, LANES), F32)

    for half in range(2):
        pieces = []
        for w in range(8):
            q = half * 8 + w
            for part in range(2):
                if q == 0:
                    before = halo[part]
                    here = x[part, :, :RAW_WINDOW]
                    pieces.append(jnp.concatenate([before, here], axis=1))
                else:
                    pieces.append(x[part, :, RAW_WINDOW * q - LANES : RAW_WINDOW * (q + 1)])
        left = jnp.concatenate(pieces, axis=0)
        out = jnp.dot(left, band[...], preferred_element_type=F32)
        for w in range(8):
            q = half * 8 + w
            rows = out[w * 32 : (w + 1) * 32]
            surv[q] = rows[:, :LANES].astype(BF16)
            at = pl.multiple_of((WINDOWS - 1 - WINDOWS_STEP * step - q) * 32, 32)
            picked[pl.ds(at, 32), :] = rows[:, LANES:]
    for part in range(2):
        halo[part] = x[part, :, WINDOWS_STEP * RAW_WINDOW - LANES :]

    @pl.when(step == STEPS - 1)
    def _():
        for k in range(TX):
            mine = lax.div(owner[k], BEAMS_HERE) == me
            local = lax.rem(owner[k], BEAMS_HERE)
            whole = lax.div(delay[k], LANES)
            rest = lax.rem(delay[k], LANES)
            turn = lax.rem(LANES - rest, LANES)
            for part in range(2):
                start = whole * 32 + part * BEAMS_HERE + local
                first = picked[pl.ds(start, WINDOWS, stride=32), :]
                second = picked[pl.ds(start + 32, WINDOWS, stride=32), :]
                moved = jnp.where(
                    lane < LANES - rest,
                    pltpu.roll(first, turn, axis=1),
                    pltpu.roll(second, turn, axis=1),
                )
                moved = jnp.where(mine, moved, 0.0).astype(BF16)
                ref[k, part * 8 : (part + 1) * 8] = moved.reshape(8, 16, LANES)


def front(voltages, surv_taps, ref_taps, tx_owner, delay_start):
    smem = pl.BlockSpec(memory_space=pltpu.SMEM)
    x = voltages.reshape(2, BEAMS_HERE, DECIM * WINDOWS * LANES)
    return pl.pallas_call(
        front_kernel,
        grid=(STEPS,),
        in_specs=[
            smem,
            smem,
            smem,
            smem,
            pl.BlockSpec((2, BEAMS_HERE, WINDOWS_STEP * RAW_WINDOW), lambda i: (0, 0, i)),
        ],
        out_specs=[
            pl.BlockSpec((WINDOWS_STEP, 32, LANES), lambda i: (i, 0, 0)),
            pl.BlockSpec((TX, BEAM, 16, LANES), lambda i: (0, 0, 0, 0)),
        ],
        out_shape=[
            jax.ShapeDtypeStruct((WINDOWS, 32, LANES), BF16),
            jax.ShapeDtypeStruct((TX, BEAM, 16, LANES), BF16),
        ],
        scratch_shapes=[
            pltpu.VMEM((5 * LANES, 2 * LANES), BF16),
            pltpu.VMEM((2, BEAMS_HERE, LANES), BF16),
            pltpu.VMEM(((WINDOWS + 8) * 32, LANES), F32),
        ],
        name="front",
    )(tx_owner, delay_start, surv_taps.astype(F32), ref_taps.astype(F32), x)


def main_kernel(
    doppler,
    surv,
    ref_in,
    roots,
    out,
    gathered,
    reduced,
    refs,
    rows,
    corr_re,
    corr_im,
    table,
    outbox,
    inbox,
    send_a,
    recv_a,
    send_b,
    recv_b,
    send_c,
    recv_c,
):
    my_beam = lax.axis_index("beam")
    my_seg = lax.axis_index("seg")

    barrier = pltpu.get_barrier_semaphore()
    for o in range(1, BEAM):
        peer = lax.rem(my_beam + o, BEAM)
        pl.semaphore_signal(barrier, inc=1, device_id={"beam": peer}, device_id_type=MESH)
    for o in range(1, SEG):
        peer = lax.rem(my_seg + o, SEG)
        pl.semaphore_signal(barrier, inc=1, device_id={"seg": peer}, device_id_type=MESH)
    pl.semaphore_wait(barrier, BEAM - 1 + SEG - 1)

    def scatter(o):
        peer = lax.rem(my_beam + o, BEAM)
        return pltpu.make_async_remote_copy(
            src_ref=ref_in.at[:, peer],
            dst_ref=gathered.at[o],
            send_sem=send_a.at[o],
            recv_sem=recv_a.at[o],
            device_id={"beam": peer},
            device_id_type=MESH,
        )

    def spread(o):
        peer = lax.rem(my_beam + o, BEAM)
        return pltpu.make_async_remote_copy(
            src_ref=reduced,
            dst_ref=refs.at[:, my_beam],
            send_sem=send_b.at[o],
            recv_sem=recv_b.at[o],
            device_id={"beam": peer},
            device_id_type=MESH,
        )

    for o in range(1, BEAM):
        scatter(o).start()
    total = ref_in[:, my_beam].astype(F32)
    for o in range(1, BEAM):
        scatter(o).wait_recv()
        total = total + gathered[o].astype(F32)
    reduced[...] = total.astype(BF16)
    for o in range(1, BEAM):
        spread(o).start()
    refs[:, my_beam] = reduced[...]
    for o in range(1, BEAM):
        spread(o).wait_recv()
    for o in range(1, BEAM):
        scatter(o).wait_send()
        spread(o).wait_send()

    for k in range(TX):
        for part in range(2):
            flat = refs[k, part * 8 : (part + 1) * 8].reshape(WINDOWS, LANES)
            rows[2 * k + part, :WINDOWS] = flat.astype(F32)
            rows[2 * k + part, WINDOWS:] = jnp.zeros((8, LANES), F32)

    lane = lax.broadcasted_iota(jnp.int32, (16, LANES), 1)
    sub = lax.broadcasted_iota(jnp.int32, (16, LANES), 0)
    low = lax.broadcasted_iota(jnp.int32, (32, LANES), 1) < BLOCK_LEN
    nil = jnp.zeros((32, LANES), BF16)

    def share(k, o):
        peer = lax.rem(my_seg + o, SEG)
        return pltpu.make_async_remote_copy(
            src_ref=outbox.at[k, peer],
            dst_ref=inbox.at[k, o],
            send_sem=send_c.at[k, o],
            recv_sem=recv_c.at[k, o],
            device_id={"seg": peer},
            device_id_type=MESH,
        )

    def staggered(kp, i):
        row = jnp.broadcast_to(rows[kp, pl.ds(i, 1), :], (8, LANES))
        top = pltpu.roll(row, 1, axis=1, stride=1, stride_axis=0)
        bottom = pltpu.roll(top, 8, axis=1)
        return jnp.concatenate([top, bottom], axis=0).astype(BF16)

    def toeplitz(below, above):
        tiles = []
        for c in range(8):
            mixed = jnp.where((lane < sub + 1) | (lane >= LANES - 16 * c), below, above)
            tiles.append(pltpu.roll(mixed, 16 * c, axis=1) if c else mixed)
        return jnp.concatenate(tiles, axis=0)

    def transmitter(k, _):
        def pair(step, _):
            stag = [
                [staggered(2 * k + part, WINDOWS - 4 * step - r) for r in range(5)]
                for part in range(2)
            ]
            for sub_q in range(2):
                quad = 2 * step + sub_q
                halves = []
                for a in range(2):
                    r = 2 * sub_q + a
                    halves.append(
                        jnp.concatenate(
                            [toeplitz(stag[part][r + 1], stag[part][r]) for part in range(2)],
                            axis=1,
                        )
                    )
                right = jnp.concatenate(halves, axis=0)
                s0 = surv[2 * quad]
                s1 = surv[2 * quad + 1]
                left = jnp.concatenate(
                    [
                        jnp.concatenate([jnp.where(low, s0, nil), nil], axis=1),
                        jnp.concatenate([jnp.where(low, nil, s0), nil], axis=1),
                        jnp.concatenate([nil, jnp.where(low, s1, nil)], axis=1),
                        jnp.concatenate([nil, jnp.where(low, nil, s1)], axis=1),
                    ],
                    axis=0,
                )
                prod = jnp.dot(left, right, preferred_element_type=F32)
                for l in range(4):
                    re = prod[32 * l : 32 * l + 16]
                    im = prod[32 * l + 16 : 32 * l + 32]
                    at = 4 * quad + l
                    corr_re[pl.ds(at, BEAMS_HERE, stride=BLOCKS), :] = re[:, :LANES] + im[:, LANES:]
                    corr_im[pl.ds(at, BEAMS_HERE, stride=BLOCKS), :] = im[:, :LANES] - re[:, LANES:]
            return 0

        lax.fori_loop(0, WINDOWS // 4, pair, 0)

        for c in range(4):
            piece = roots[pl.ds(4 * doppler[k] + c, DOPPLER, stride=4), :].astype(BF16)
            table[:DOPPLER, c * LANES : (c + 1) * LANES] = piece
            if c < 2:
                table[DOPPLER:, BLOCKS + c * LANES : BLOCKS + (c + 1) * LANES] = piece
            else:
                table[DOPPLER:, (c - 2) * LANES : (c - 1) * LANES] = -piece

        def beams(bp, _):
            at = pl.multiple_of(bp * 2 * BLOCKS, 2 * BLOCKS)
            re = corr_re[pl.ds(at, 2 * BLOCKS), :].astype(BF16)
            im = corr_im[pl.ds(at, 2 * BLOCKS), :].astype(BF16)
            right = jnp.concatenate(
                [
                    jnp.concatenate([re[:BLOCKS], re[BLOCKS:]], axis=1),
                    jnp.concatenate([im[:BLOCKS], im[BLOCKS:]], axis=1),
                ],
                axis=0,
            )
            spec = jnp.dot(table[...], right, preferred_element_type=F32)
            sre, sim = spec[:DOPPLER], spec[DOPPLER:]
            power = (sre * sre + sim * sim) * (1.0 / (4 * BLOCKS * BLOCK_LEN))
            for b in range(2):
                turned = power[:, b * LANES : (b + 1) * LANES].T.astype(BF16)
                for g in range(SEG):
                    outbox[k, g, 2 * bp + b] = turned[16 * g : 16 * (g + 1)]
            return 0

        lax.fori_loop(0, BEAMS_HERE // 2, beams, 0)
        for o in range(1, SEG):
            share(k, o).start()
        return 0

    lax.fori_loop(0, TX, transmitter, 0)

    def collect(k, _):
        total = outbox[k, my_seg].astype(F32)
        for o in range(1, SEG):
            share(k, o).wait_recv()
            total = total + inbox[k, o].astype(F32)
        out[k] = total * (1.0 / SEG)
        for o in range(1, SEG):
            share(k, o).wait_send()
        return 0

    lax.fori_loop(0, TX, collect, 0)


def root_table():
    ells = np.arange(BLOCKS)[None, :]
    freqs = np.arange(2 * DOPPLER)[:, None] - BLOCKS // 2
    angle = 2.0 * np.pi / BLOCKS * ((ells * freqs) % BLOCKS)
    both = np.concatenate([np.cos(angle), np.sin(angle)], axis=1)
    return jnp.asarray(both.reshape(8 * DOPPLER, LANES), F32)


def ambiguity(doppler_start, surv, ref):
    vmem = pl.BlockSpec(memory_space=pltpu.VMEM)
    return pl.pallas_call(
        main_kernel,
        in_specs=[pl.BlockSpec(memory_space=pltpu.SMEM), vmem, vmem, vmem],
        out_specs=vmem,
        out_shape=jax.ShapeDtypeStruct((TX, BEAMS_HERE, DELAYS // SEG, DOPPLER), F32),
        scratch_shapes=[
            pltpu.VMEM((BEAM, TX, 16, LANES), BF16),
            pltpu.VMEM((TX, 16, LANES), BF16),
            pltpu.VMEM((TX, BEAM, 16, LANES), BF16),
            pltpu.VMEM((2 * TX, WINDOWS + 8, LANES), F32),
            pltpu.VMEM((BEAMS_HERE * BLOCKS, LANES), F32),
            pltpu.VMEM((BEAMS_HERE * BLOCKS, LANES), F32),
            pltpu.VMEM((2 * DOPPLER, 2 * BLOCKS), BF16),
            pltpu.VMEM((TX, SEG, BEAMS_HERE, 16, LANES), BF16),
            pltpu.VMEM((TX, SEG, BEAMS_HERE, 16, LANES), BF16),
            pltpu.SemaphoreType.DMA((BEAM,)),
            pltpu.SemaphoreType.DMA((BEAM,)),
            pltpu.SemaphoreType.DMA((BEAM,)),
            pltpu.SemaphoreType.DMA((BEAM,)),
            pltpu.SemaphoreType.DMA((TX, SEG)),
            pltpu.SemaphoreType.DMA((TX, SEG)),
        ],
        compiler_params=pltpu.CompilerParams(collective_id=0, has_side_effects=True),
        name="ambiguity",
    )(doppler_start, surv, ref, root_table())


def shards(voltages, surv_taps, ref_taps, tx_owner, delay_start, doppler_start):
    surv, ref = front(voltages, surv_taps, ref_taps, tx_owner, delay_start)
    return ambiguity(doppler_start, surv, ref)


def solution(mesh):
    return jax.shard_map(
        shards,
        mesh=mesh,
        in_specs=(P(None, "beam", "seg", None), P(), P(), P(), P(), P()),
        out_specs=P(None, "beam", "seg", None),
        check_vma=False,
    )
```

```python
import functools

import jax
import jax.numpy as jnp
import numpy as np
from jax import lax
from jax.experimental import pallas as pl
from jax.experimental.pallas import tpu as pltpu
from jax.sharding import PartitionSpec as P

TX = 4
DECIM = 4
TAPS = 32
BLOCK_LEN = 64
BLOCKS = 256
DELAYS = 128
DOPPLER = 128
LANES = 128
BEAMS_HERE = 16
WINDOWS = 128
WINDOWS_STEP = 32
STEPS = WINDOWS // WINDOWS_STEP
RAW_WINDOW = DECIM * LANES
REGION = (WINDOWS + 8) * 8
BEAM = 16
SEG = 8
QUADS = 64
F32 = jnp.float32
BF16 = jnp.bfloat16
MESH = pl.DeviceIdType.MESH


def band_base(taps, backwards):
    rows = lax.broadcasted_iota(jnp.int32, (LANES, LANES), 0)
    cols = lax.broadcasted_iota(jnp.int32, (LANES, LANES), 1)
    if backwards:
        cols = LANES - 1 - cols
    offset = DECIM * cols - rows
    total = jnp.zeros((LANES, LANES), F32)
    for tap in range(TAPS):
        total = jnp.where(offset == tap, taps[tap].astype(F32), total)
    return total


def front_kernel(owner, delay, surv_taps, ref_taps, x, surv, ref, band, halo, picked):
    step = pl.program_id(0)
    me = lax.axis_index("beam")
    lane = lax.broadcasted_iota(jnp.int32, (LANES, LANES), 1)

    @pl.when(step == 0)
    def _():
        forward = band_base(surv_taps, False)
        backward = band_base(ref_taps, True)
        for part in range(5):
            shift = 32 * (part - 1)
            ahead = pltpu.roll(forward, shift % LANES, axis=1)
            behind = pltpu.roll(backward, -shift % LANES, axis=1)
            if part == 0:
                ahead = jnp.where(lane < 8, ahead, 0.0)
                behind = jnp.where(lane >= LANES - 8, behind, 0.0)
            else:
                ahead = jnp.where(lane >= shift, ahead, 0.0)
                behind = jnp.where(lane < LANES - shift, behind, 0.0)
            band[part * LANES : (part + 1) * LANES, :LANES] = ahead.astype(BF16)
            band[part * LANES : (part + 1) * LANES, LANES:] = behind.astype(BF16)
        halo[...] = jnp.zeros_like(halo)
        for r in range(4):
            picked[r * REGION + WINDOWS * 8 : (r + 1) * REGION, :] = jnp.zeros((64, LANES), F32)

    for half in range(WINDOWS_STEP // 8):
        pieces = []
        for w in range(8):
            q = half * 8 + w
            for part in range(2):
                if q == 0:
                    before = halo[part]
                    here = x[part, :, :RAW_WINDOW]
                    pieces.append(jnp.concatenate([before, here], axis=1))
                else:
                    pieces.append(x[part, :, RAW_WINDOW * q - LANES : RAW_WINDOW * (q + 1)])
        left = jnp.concatenate(pieces, axis=0)
        out = jnp.dot(left, band[...], preferred_element_type=F32)
        for w in range(8):
            q = half * 8 + w
            rows = out[w * 32 : (w + 1) * 32]
            surv[q] = rows[:, :LANES].astype(BF16)
            at = pl.multiple_of((WINDOWS - 1 - WINDOWS_STEP * step - q) * 8, 8)
            for r in range(4):
                picked[pl.ds(at + r * REGION, 8), :] = rows[8 * r : 8 * r + 8, LANES:]
    for part in range(2):
        halo[part] = x[part, :, WINDOWS_STEP * RAW_WINDOW - LANES :]

    @pl.when(step == STEPS - 1)
    def _():
        for k in range(TX):
            mine = lax.div(owner[k], BEAMS_HERE) == me
            local = lax.rem(owner[k], BEAMS_HERE)
            whole = lax.div(delay[k], LANES)
            rest = lax.rem(delay[k], LANES)
            turn = lax.rem(LANES - rest, LANES)
            for part in range(2):
                start = (2 * part + lax.div(local, 8)) * REGION + whole * 8 + lax.rem(local, 8)
                first = picked[pl.ds(start, WINDOWS, stride=8), :]
                second = picked[pl.ds(start + 8, WINDOWS, stride=8), :]
                moved = jnp.where(
                    lane < LANES - rest,
                    pltpu.roll(first, turn, axis=1),
                    pltpu.roll(second, turn, axis=1),
                )
                moved = jnp.where(mine, moved, 0.0).astype(BF16)
                ref[k, part * 8 : (part + 1) * 8] = moved.reshape(8, 16, LANES)


def front(voltages, surv_taps, ref_taps, tx_owner, delay_start):
    smem = pl.BlockSpec(memory_space=pltpu.SMEM)
    x = voltages.reshape(2, BEAMS_HERE, DECIM * WINDOWS * LANES)
    return pl.pallas_call(
        front_kernel,
        grid=(STEPS,),
        in_specs=[
            smem,
            smem,
            smem,
            smem,
            pl.BlockSpec((2, BEAMS_HERE, WINDOWS_STEP * RAW_WINDOW), lambda i: (0, 0, i)),
        ],
        out_specs=[
            pl.BlockSpec((WINDOWS_STEP, 32, LANES), lambda i: (i, 0, 0)),
            pl.BlockSpec((TX, BEAM, 16, LANES), lambda i: (0, 0, 0, 0)),
        ],
        out_shape=[
            jax.ShapeDtypeStruct((WINDOWS, 32, LANES), BF16),
            jax.ShapeDtypeStruct((TX, BEAM, 16, LANES), BF16),
        ],
        scratch_shapes=[
            pltpu.VMEM((5 * LANES, 2 * LANES), BF16),
            pltpu.VMEM((2, BEAMS_HERE, LANES), BF16),
            pltpu.VMEM((4 * REGION, LANES), F32),
        ],
        name="front",
    )(tx_owner, delay_start, surv_taps, ref_taps, x)


def main_kernel(
    doppler,
    surv,
    ref_in,
    roots,
    out,
    gathered,
    reduced,
    refs,
    rows,
    corr_re,
    corr_im,
    table,
    outbox,
    inbox,
    send_a,
    recv_a,
    send_b,
    recv_b,
    send_c,
    recv_c,
):
    my_beam = lax.axis_index("beam")
    my_seg = lax.axis_index("seg")

    barrier = pltpu.get_barrier_semaphore()
    for o in range(1, BEAM):
        peer = lax.rem(my_beam + o, BEAM)
        pl.semaphore_signal(barrier, inc=1, device_id={"beam": peer}, device_id_type=MESH)
    for o in range(1, SEG):
        peer = lax.rem(my_seg + o, SEG)
        pl.semaphore_signal(barrier, inc=1, device_id={"seg": peer}, device_id_type=MESH)
    pl.semaphore_wait(barrier, BEAM - 1 + SEG - 1)

    def scatter(o):
        peer = lax.rem(my_beam + o, BEAM)
        return pltpu.make_async_remote_copy(
            src_ref=ref_in.at[:, peer],
            dst_ref=gathered.at[o],
            send_sem=send_a.at[o],
            recv_sem=recv_a.at[o],
            device_id={"beam": peer},
            device_id_type=MESH,
        )

    def spread(o):
        peer = lax.rem(my_beam + o, BEAM)
        return pltpu.make_async_remote_copy(
            src_ref=reduced,
            dst_ref=refs.at[:, my_beam],
            send_sem=send_b.at[o],
            recv_sem=recv_b.at[o],
            device_id={"beam": peer},
            device_id_type=MESH,
        )

    for o in range(1, BEAM):
        scatter(o).start()
    total = ref_in[:, my_beam].astype(F32)
    for o in range(1, BEAM):
        scatter(o).wait_recv()
        total = total + gathered[o].astype(F32)
    reduced[...] = total.astype(BF16)
    for o in range(1, BEAM):
        spread(o).start()
    refs[:, my_beam] = reduced[...]
    for o in range(1, BEAM):
        spread(o).wait_recv()
    for o in range(1, BEAM):
        scatter(o).wait_send()
        spread(o).wait_send()

    for k in range(TX):
        for part in range(2):
            flat = refs[k, part * 8 : (part + 1) * 8].reshape(WINDOWS, LANES)
            rows[2 * k + part, :WINDOWS] = flat.astype(F32)
            rows[2 * k + part, WINDOWS:] = jnp.zeros((8, LANES), F32)

    lane = lax.broadcasted_iota(jnp.int32, (16, LANES), 1)
    sub = lax.broadcasted_iota(jnp.int32, (16, LANES), 0)
    low = lax.broadcasted_iota(jnp.int32, (32, LANES), 1) < BLOCK_LEN
    nil = jnp.zeros((32, LANES), BF16)

    def share(k, o):
        peer = lax.rem(my_seg + o, SEG)
        return pltpu.make_async_remote_copy(
            src_ref=outbox.at[k, peer],
            dst_ref=inbox.at[k, o],
            send_sem=send_c.at[k, o],
            recv_sem=recv_c.at[k, o],
            device_id={"seg": peer},
            device_id_type=MESH,
        )

    def staggered(kp, i):
        row = jnp.broadcast_to(rows[kp, pl.ds(i, 1), :], (8, LANES))
        top = pltpu.roll(row, 1, axis=1, stride=1, stride_axis=0)
        bottom = pltpu.roll(top, 8, axis=1)
        return jnp.concatenate([top, bottom], axis=0).astype(BF16)

    def toeplitz(below, above):
        tiles = []
        for c in range(8):
            mixed = jnp.where((lane < sub + 1) | (lane >= LANES - 16 * c), below, above)
            tiles.append(pltpu.roll(mixed, 16 * c, axis=1) if c else mixed)
        return jnp.concatenate(tiles, axis=0)

    def transmitter(k, _):
        def pair(step, _):
            stag = [
                [staggered(2 * k + part, WINDOWS - 2 * QUADS * step - r) for r in range(2 * QUADS + 1)]
                for part in range(2)
            ]
            for sub_q in range(QUADS):
                quad = QUADS * step + sub_q
                halves = []
                for a in range(2):
                    r = 2 * sub_q + a
                    halves.append(
                        jnp.concatenate(
                            [toeplitz(stag[part][r + 1], stag[part][r]) for part in range(2)],
                            axis=1,
                        )
                    )
                right = jnp.concatenate(halves, axis=0)
                s0 = surv[2 * quad]
                s1 = surv[2 * quad + 1]
                left = jnp.concatenate(
                    [
                        jnp.concatenate([jnp.where(low, s0, nil), nil], axis=1),
                        jnp.concatenate([jnp.where(low, nil, s0), nil], axis=1),
                        jnp.concatenate([nil, jnp.where(low, s1, nil)], axis=1),
                        jnp.concatenate([nil, jnp.where(low, nil, s1)], axis=1),
                    ],
                    axis=0,
                )
                prod = jnp.dot(left, right, preferred_element_type=F32)
                for l in range(4):
                    re = prod[32 * l : 32 * l + 16]
                    im = prod[32 * l + 16 : 32 * l + 32]
                    cre = re[:, :LANES] + im[:, LANES:]
                    cim = im[:, :LANES] - re[:, LANES:]
                    for half in range(2):
                        at = pl.multiple_of((4 * quad + l) * 8, 8) + half * 8 * BLOCKS
                        corr_re[pl.ds(at, 8), :] = cre[8 * half : 8 * half + 8]
                        corr_im[pl.ds(at, 8), :] = cim[8 * half : 8 * half + 8]
            return 0

        lax.fori_loop(0, WINDOWS // (2 * QUADS), pair, 0)

        for c in range(4):
            piece = roots[pl.ds(4 * doppler[k] + c, DOPPLER, stride=4), :].astype(BF16)
            table[:DOPPLER, c * LANES : (c + 1) * LANES] = piece
            if c < 2:
                table[DOPPLER:, BLOCKS + c * LANES : BLOCKS + (c + 1) * LANES] = piece
            else:
                table[DOPPLER:, (c - 2) * LANES : (c - 1) * LANES] = -piece

        def beams(half, _):
            def column(ref, b):
                at = half * 8 * BLOCKS + b
                return ref[pl.ds(at, BLOCKS, stride=8), :].astype(BF16)

            for bp in range(4):
                right = jnp.concatenate(
                    [
                        jnp.concatenate([column(ref, 2 * bp), column(ref, 2 * bp + 1)], axis=1)
                        for ref in (corr_re, corr_im)
                    ],
                    axis=0,
                )
                spec = jnp.dot(table[...], right, preferred_element_type=F32)
                sre, sim = spec[:DOPPLER], spec[DOPPLER:]
                power = (sre * sre + sim * sim) * (1.0 / (4 * BLOCKS * BLOCK_LEN))
                for b in range(2):
                    turned = power[:, b * LANES : (b + 1) * LANES].T.astype(BF16)
                    for g in range(SEG):
                        outbox[k, g, 8 * half + 2 * bp + b] = turned[16 * g : 16 * (g + 1)]
            return 0

        lax.fori_loop(0, 2, beams, 0)
        for o in range(1, SEG):
            share(k, o).start()
        return 0

    lax.fori_loop(0, TX, transmitter, 0)

    def collect(k, _):
        total = outbox[k, my_seg].astype(F32)
        for o in range(1, SEG):
            share(k, o).wait_recv()
            total = total + inbox[k, o].astype(F32)
        out[k] = total * (1.0 / SEG)
        for o in range(1, SEG):
            share(k, o).wait_send()
        return 0

    lax.fori_loop(0, TX, collect, 0)


def root_table():
    ells = np.arange(BLOCKS)[None, :]
    freqs = np.arange(2 * DOPPLER)[:, None] - BLOCKS // 2
    angle = 2.0 * np.pi / BLOCKS * ((ells * freqs) % BLOCKS)
    both = np.concatenate([np.cos(angle), np.sin(angle)], axis=1)
    return jnp.asarray(both.reshape(8 * DOPPLER, LANES), F32)


def ambiguity(doppler_start, surv, ref):
    vmem = pl.BlockSpec(memory_space=pltpu.VMEM)
    return pl.pallas_call(
        main_kernel,
        in_specs=[pl.BlockSpec(memory_space=pltpu.SMEM), vmem, vmem, vmem],
        out_specs=vmem,
        out_shape=jax.ShapeDtypeStruct((TX, BEAMS_HERE, DELAYS // SEG, DOPPLER), F32),
        scratch_shapes=[
            pltpu.VMEM((BEAM, TX, 16, LANES), BF16),
            pltpu.VMEM((TX, 16, LANES), BF16),
            pltpu.VMEM((TX, BEAM, 16, LANES), BF16),
            pltpu.VMEM((2 * TX, WINDOWS + 8, LANES), F32),
            pltpu.VMEM((BEAMS_HERE * BLOCKS, LANES), F32),
            pltpu.VMEM((BEAMS_HERE * BLOCKS, LANES), F32),
            pltpu.VMEM((2 * DOPPLER, 2 * BLOCKS), BF16),
            pltpu.VMEM((TX, SEG, BEAMS_HERE, 16, LANES), BF16),
            pltpu.VMEM((TX, SEG, BEAMS_HERE, 16, LANES), BF16),
            pltpu.SemaphoreType.DMA((BEAM,)),
            pltpu.SemaphoreType.DMA((BEAM,)),
            pltpu.SemaphoreType.DMA((BEAM,)),
            pltpu.SemaphoreType.DMA((BEAM,)),
            pltpu.SemaphoreType.DMA((TX, SEG)),
            pltpu.SemaphoreType.DMA((TX, SEG)),
        ],
        compiler_params=pltpu.CompilerParams(collective_id=0, has_side_effects=True),
        name="ambiguity",
    )(doppler_start, surv, ref, root_table())


def shards(voltages, surv_taps, ref_taps, tx_owner, delay_start, doppler_start):
    surv, ref = front(voltages, surv_taps, ref_taps, tx_owner, delay_start)
    return ambiguity(doppler_start, surv, ref)


def solution(mesh):
    return jax.shard_map(
        shards,
        mesh=mesh,
        in_specs=(P(None, "beam", "seg", None), P(), P(), P(), P(), P()),
        out_specs=P(None, "beam", "seg", None),
        check_vma=False,
    )
```

```python
import functools

import jax
import jax.numpy as jnp
import numpy as np
from jax import lax
from jax.experimental import pallas as pl
from jax.experimental.pallas import tpu as pltpu
from jax.sharding import PartitionSpec as P

TX = 4
DECIM = 4
TAPS = 32
BLOCK_LEN = 64
BLOCKS = 256
DELAYS = 128
DOPPLER = 128
LANES = 128
BEAMS_HERE = 16
WINDOWS = 128
WINDOWS_STEP = 32
CHUNK = WINDOWS_STEP * 512
STEPS = WINDOWS // WINDOWS_STEP
RAW_WINDOW = DECIM * LANES
REGION = (WINDOWS + 8) * 8
BEAM = 16
SEG = 8
QUADS = 64
F32 = jnp.float32
BF16 = jnp.bfloat16
MESH = pl.DeviceIdType.MESH


def band_base(taps, backwards):
    rows = lax.broadcasted_iota(jnp.int32, (LANES, LANES), 0)
    cols = lax.broadcasted_iota(jnp.int32, (LANES, LANES), 1)
    if backwards:
        cols = LANES - 1 - cols
    offset = DECIM * cols - rows
    total = jnp.zeros((LANES, LANES), F32)
    for tap in range(TAPS):
        total = jnp.where(offset == tap, taps[tap].astype(F32), total)
    return total


def main_kernel(
    owner,
    delay,
    doppler,
    surv_taps,
    ref_taps,
    x_hbm,
    roots_hbm,
    out,
    x,
    roots,
    band,
    surv,
    picked,
    ref_in,
    gathered,
    reduced,
    refs,
    rows,
    corr_re,
    corr_im,
    table,
    outbox,
    inbox,
    sem_x,
    sem_roots,
    send_a,
    recv_a,
    send_b,
    recv_b,
    send_c,
    recv_c,
):
    my_beam = lax.axis_index("beam")
    my_seg = lax.axis_index("seg")

    def fetch(c):
        at = pl.multiple_of(c * CHUNK, LANES)
        return pltpu.make_async_copy(
            x_hbm.at[:, :, pl.ds(at, CHUNK)],
            x.at[:, :, pl.ds(at + LANES, CHUNK)],
            sem_x.at[c],
        )

    for c in range(STEPS):
        fetch(c).start()
    fetch_roots = pltpu.make_async_copy(roots_hbm, roots, sem_roots)
    fetch_roots.start()

    barrier = pltpu.get_barrier_semaphore()
    for o in range(1, BEAM):
        peer = lax.rem(my_beam + o, BEAM)
        pl.semaphore_signal(barrier, inc=1, device_id={"beam": peer}, device_id_type=MESH)
    for o in range(1, SEG):
        peer = lax.rem(my_seg + o, SEG)
        pl.semaphore_signal(barrier, inc=1, device_id={"seg": peer}, device_id_type=MESH)

    wide = lax.broadcasted_iota(jnp.int32, (LANES, LANES), 1)
    forward = band_base(surv_taps, False)
    backward = band_base(ref_taps, True)
    for part in range(5):
        shift = 32 * (part - 1)
        ahead = pltpu.roll(forward, shift % LANES, axis=1)
        behind = pltpu.roll(backward, -shift % LANES, axis=1)
        if part == 0:
            ahead = jnp.where(wide < 8, ahead, 0.0)
            behind = jnp.where(wide >= LANES - 8, behind, 0.0)
        else:
            ahead = jnp.where(wide >= shift, ahead, 0.0)
            behind = jnp.where(wide < LANES - shift, behind, 0.0)
        band[part * LANES : (part + 1) * LANES, :LANES] = ahead.astype(BF16)
        band[part * LANES : (part + 1) * LANES, LANES:] = behind.astype(BF16)
    x[:, :, :LANES] = jnp.zeros((2, BEAMS_HERE, LANES), BF16)
    for r in range(4):
        picked[r * REGION + WINDOWS * 8 : (r + 1) * REGION, :] = jnp.zeros((64, LANES), F32)

    def decimate(step, _):
        fetch(step).wait()
        for group in range(WINDOWS_STEP // 8):
            pieces = []
            for w in range(8):
                q = step * WINDOWS_STEP + group * 8 + w
                at = pl.multiple_of(q * RAW_WINDOW, LANES)
                for part in range(2):
                    pieces.append(x[part, :, pl.ds(at, RAW_WINDOW + LANES)])
            left = jnp.concatenate(pieces, axis=0)
            both = jnp.dot(left, band[...], preferred_element_type=F32)
            for w in range(8):
                q = step * WINDOWS_STEP + group * 8 + w
                part_rows = both[w * 32 : (w + 1) * 32]
                surv[q] = part_rows[:, :LANES].astype(BF16)
                at = pl.multiple_of((WINDOWS - 1 - q) * 8, 8)
                for r in range(4):
                    picked[pl.ds(at + r * REGION, 8), :] = part_rows[8 * r : 8 * r + 8, LANES:]
        return 0

    lax.fori_loop(0, STEPS, decimate, 0)

    def pick(k):
        mine = lax.div(owner[k], BEAMS_HERE) == my_beam
        local = lax.rem(owner[k], BEAMS_HERE)
        whole = lax.div(delay[k], LANES)
        rest = lax.rem(delay[k], LANES)
        turn = lax.rem(LANES - rest, LANES)
        for part in range(2):
            start = (2 * part + lax.div(local, 8)) * REGION + whole * 8 + lax.rem(local, 8)
            first = picked[pl.ds(start, WINDOWS, stride=8), :]
            second = picked[pl.ds(start + 8, WINDOWS, stride=8), :]
            moved = jnp.where(
                wide < LANES - rest,
                pltpu.roll(first, turn, axis=1),
                pltpu.roll(second, turn, axis=1),
            )
            moved = jnp.where(mine, moved, 0.0).astype(BF16)
            ref_in[k, part * 8 : (part + 1) * 8] = moved.reshape(8, 16, LANES)

    groups = ((0, 1), (1, 3))

    def scatter(g, o):
        base, count = groups[g]
        peer = lax.rem(my_beam + o, BEAM)
        return pltpu.make_async_remote_copy(
            src_ref=ref_in.at[pl.ds(base, count), peer],
            dst_ref=gathered.at[o, pl.ds(base, count)],
            send_sem=send_a.at[g, o],
            recv_sem=recv_a.at[g, o],
            device_id={"beam": peer},
            device_id_type=MESH,
        )

    def spread(g, o):
        base, count = groups[g]
        peer = lax.rem(my_beam + o, BEAM)
        return pltpu.make_async_remote_copy(
            src_ref=reduced.at[pl.ds(base, count)],
            dst_ref=refs.at[pl.ds(base, count), my_beam],
            send_sem=send_b.at[g, o],
            recv_sem=recv_b.at[g, o],
            device_id={"beam": peer},
            device_id_type=MESH,
        )

    def spread_sums(g):
        base, count = groups[g]
        total = ref_in[base : base + count, my_beam].astype(F32)
        for o in range(1, BEAM):
            scatter(g, o).wait_recv()
            total = total + gathered[o, base : base + count].astype(F32)
        reduced[base : base + count] = total.astype(BF16)
        for o in range(1, BEAM):
            spread(g, o).start()
        refs[base : base + count, my_beam] = reduced[base : base + count]

    def arrive(g):
        base, count = groups[g]
        for o in range(1, BEAM):
            spread(g, o).wait_recv()
        for k in range(base, base + count):
            for part in range(2):
                flat = refs[k, part * 8 : (part + 1) * 8].reshape(WINDOWS, LANES)
                rows[2 * k + part, :WINDOWS] = flat.astype(F32)
                rows[2 * k + part, WINDOWS:] = jnp.zeros((8, LANES), F32)

    pick(0)
    pl.semaphore_wait(barrier, BEAM - 1 + SEG - 1)
    for o in range(1, BEAM):
        scatter(0, o).start()
    for k in range(1, TX):
        pick(k)
    for o in range(1, BEAM):
        scatter(1, o).start()
    fetch_roots.wait()
    spread_sums(0)
    spread_sums(1)
    arrive(0)

    lane = lax.broadcasted_iota(jnp.int32, (16, LANES), 1)
    sub = lax.broadcasted_iota(jnp.int32, (16, LANES), 0)
    low = lax.broadcasted_iota(jnp.int32, (32, LANES), 1) < BLOCK_LEN
    nil = jnp.zeros((32, LANES), BF16)

    def share(k, half, o):
        peer = lax.rem(my_seg + o, SEG)
        at = pl.multiple_of(half * 8, 8)
        return pltpu.make_async_remote_copy(
            src_ref=outbox.at[k, peer, pl.ds(at, 8)],
            dst_ref=inbox.at[k, o, pl.ds(at, 8)],
            send_sem=send_c.at[k, half, o],
            recv_sem=recv_c.at[k, half, o],
            device_id={"seg": peer},
            device_id_type=MESH,
        )

    def staggered(kp, i):
        row = jnp.broadcast_to(rows[kp, pl.ds(i, 1), :], (8, LANES))
        top = pltpu.roll(row, 1, axis=1, stride=1, stride_axis=0)
        bottom = pltpu.roll(top, 8, axis=1)
        return jnp.concatenate([top, bottom], axis=0).astype(BF16)

    def toeplitz(below, above):
        tiles = []
        for c in range(8):
            mixed = jnp.where((lane < sub + 1) | (lane >= LANES - 16 * c), below, above)
            tiles.append(pltpu.roll(mixed, 16 * c, axis=1) if c else mixed)
        return jnp.concatenate(tiles, axis=0)

    def transmitter(k, _):
        def pair(step, _):
            stag = [
                [staggered(2 * k + part, WINDOWS - 2 * QUADS * step - r) for r in range(2 * QUADS + 1)]
                for part in range(2)
            ]
            for sub_q in range(QUADS):
                quad = QUADS * step + sub_q
                halves = []
                for a in range(2):
                    r = 2 * sub_q + a
                    halves.append(
                        jnp.concatenate(
                            [toeplitz(stag[part][r + 1], stag[part][r]) for part in range(2)],
                            axis=1,
                        )
                    )
                right = jnp.concatenate(halves, axis=0)
                s0 = surv[2 * quad]
                s1 = surv[2 * quad + 1]
                left = jnp.concatenate(
                    [
                        jnp.concatenate([jnp.where(low, s0, nil), nil], axis=1),
                        jnp.concatenate([jnp.where(low, nil, s0), nil], axis=1),
                        jnp.concatenate([nil, jnp.where(low, s1, nil)], axis=1),
                        jnp.concatenate([nil, jnp.where(low, nil, s1)], axis=1),
                    ],
                    axis=0,
                )
                prod = jnp.dot(left, right, preferred_element_type=F32)
                for l in range(4):
                    re = prod[32 * l : 32 * l + 16]
                    im = prod[32 * l + 16 : 32 * l + 32]
                    cre = re[:, :LANES] + im[:, LANES:]
                    cim = im[:, :LANES] - re[:, LANES:]
                    for half in range(2):
                        at = pl.multiple_of((4 * quad + l) * 8, 8) + half * 8 * BLOCKS
                        corr_re[pl.ds(at, 8), :] = cre[8 * half : 8 * half + 8]
                        corr_im[pl.ds(at, 8), :] = cim[8 * half : 8 * half + 8]
            return 0

        lax.fori_loop(0, WINDOWS // (2 * QUADS), pair, 0)

        for c in range(4):
            piece = roots[pl.ds(4 * doppler[k] + c, DOPPLER, stride=4), :].astype(BF16)
            table[:DOPPLER, c * LANES : (c + 1) * LANES] = piece
            if c < 2:
                table[DOPPLER:, BLOCKS + c * LANES : BLOCKS + (c + 1) * LANES] = piece
            else:
                table[DOPPLER:, (c - 2) * LANES : (c - 1) * LANES] = -piece

        def beams(half, _):
            def column(ref, b):
                at = half * 8 * BLOCKS + b
                return ref[pl.ds(at, BLOCKS, stride=8), :].astype(BF16)

            for bp in range(4):
                right = jnp.concatenate(
                    [
                        jnp.concatenate([column(ref, 2 * bp), column(ref, 2 * bp + 1)], axis=1)
                        for ref in (corr_re, corr_im)
                    ],
                    axis=0,
                )
                spec = jnp.dot(table[...], right, preferred_element_type=F32)
                sre, sim = spec[:DOPPLER], spec[DOPPLER:]
                power = (sre * sre + sim * sim) * (1.0 / (4 * BLOCKS * BLOCK_LEN))
                for b in range(2):
                    turned = power[:, b * LANES : (b + 1) * LANES].T.astype(BF16)
                    for g in range(SEG):
                        outbox[k, g, 8 * half + 2 * bp + b] = turned[16 * g : 16 * (g + 1)]
            for o in range(1, SEG):
                share(k, half, o).start()
            return 0

        lax.fori_loop(0, 2, beams, 0)

        @pl.when(k == 0)
        def _():
            arrive(1)

        return 0

    lax.fori_loop(0, TX, transmitter, 0)

    for g in range(2):
        for o in range(1, BEAM):
            scatter(g, o).wait_send()
            spread(g, o).wait_send()

    def collect(k, _):
        for half in range(2):
            beams_half = slice(8 * half, 8 * half + 8)
            total = outbox[k, my_seg, beams_half].astype(F32)
            for o in range(1, SEG):
                share(k, half, o).wait_recv()
                total = total + inbox[k, o, beams_half].astype(F32)
            out[k, beams_half] = total * (1.0 / SEG)
            for o in range(1, SEG):
                share(k, half, o).wait_send()
        return 0

    lax.fori_loop(0, TX, collect, 0)


def root_table():
    ells = np.arange(BLOCKS)[None, :]
    freqs = np.arange(2 * DOPPLER)[:, None] - BLOCKS // 2
    angle = 2.0 * np.pi / BLOCKS * ((ells * freqs) % BLOCKS)
    both = np.concatenate([np.cos(angle), np.sin(angle)], axis=1)
    return jnp.asarray(both.reshape(8 * DOPPLER, LANES), F32)


def shards(voltages, surv_taps, ref_taps, tx_owner, delay_start, doppler_start):
    smem = pl.BlockSpec(memory_space=pltpu.SMEM)
    hbm = pl.BlockSpec(memory_space=pl.ANY)
    dma = pltpu.SemaphoreType.DMA
    raw = DECIM * WINDOWS * LANES
    return pl.pallas_call(
        main_kernel,
        in_specs=[smem] * 5 + [hbm] * 2,
        out_specs=pl.BlockSpec(memory_space=pltpu.VMEM),
        out_shape=jax.ShapeDtypeStruct((TX, BEAMS_HERE, DELAYS // SEG, DOPPLER), F32),
        scratch_shapes=[
            pltpu.VMEM((2, BEAMS_HERE, raw + LANES), BF16),
            pltpu.VMEM((8 * DOPPLER, LANES), F32),
            pltpu.VMEM((5 * LANES, 2 * LANES), BF16),
            pltpu.VMEM((WINDOWS, 32, LANES), BF16),
            pltpu.VMEM((4 * REGION, LANES), F32),
            pltpu.VMEM((TX, BEAM, 16, LANES), BF16),
            pltpu.VMEM((BEAM, TX, 16, LANES), BF16),
            pltpu.VMEM((TX, 16, LANES), BF16),
            pltpu.VMEM((TX, BEAM, 16, LANES), BF16),
            pltpu.VMEM((2 * TX, WINDOWS + 8, LANES), F32),
            pltpu.VMEM((BEAMS_HERE * BLOCKS, LANES), F32),
            pltpu.VMEM((BEAMS_HERE * BLOCKS, LANES), F32),
            pltpu.VMEM((2 * DOPPLER, 2 * BLOCKS), BF16),
            pltpu.VMEM((TX, SEG, BEAMS_HERE, 16, LANES), BF16),
            pltpu.VMEM((TX, SEG, BEAMS_HERE, 16, LANES), BF16),
            dma((STEPS,)),
            dma,
            dma((2, BEAM)),
            dma((2, BEAM)),
            dma((2, BEAM)),
            dma((2, BEAM)),
            dma((TX, 2, SEG)),
            dma((TX, 2, SEG)),
        ],
        compiler_params=pltpu.CompilerParams(collective_id=0, has_side_effects=True),
        name="ambiguity",
    )(
        tx_owner,
        delay_start,
        doppler_start,
        surv_taps,
        ref_taps,
        voltages.reshape(2, BEAMS_HERE, raw),
        root_table(),
    )


def solution(mesh):
    return jax.shard_map(
        shards,
        mesh=mesh,
        in_specs=(P(None, "beam", "seg", None), P(), P(), P(), P(), P()),
        out_specs=P(None, "beam", "seg", None),
        check_vma=False,
    )
```

```python
import functools

import jax
import jax.numpy as jnp
import numpy as np
from jax import lax
from jax.experimental import pallas as pl
from jax.experimental.pallas import tpu as pltpu
from jax.sharding import PartitionSpec as P

TX = 4
DECIM = 4
TAPS = 32
BLOCK_LEN = 64
BLOCKS = 256
DELAYS = 128
DOPPLER = 128
LANES = 128
BEAMS_HERE = 16
WINDOWS = 128
WINDOWS_STEP = 32
CHUNK = WINDOWS_STEP * 512
STEPS = WINDOWS // WINDOWS_STEP
RAW_WINDOW = DECIM * LANES
REGION = (WINDOWS + 8) * 8
BEAM = 16
SEG = 8
QUADS = 64
F32 = jnp.float32
BF16 = jnp.bfloat16
MESH = pl.DeviceIdType.MESH


def band_base(taps, backwards):
    rows = lax.broadcasted_iota(jnp.int32, (LANES, LANES), 0)
    cols = lax.broadcasted_iota(jnp.int32, (LANES, LANES), 1)
    if backwards:
        cols = LANES - 1 - cols
    offset = DECIM * cols - rows
    total = jnp.zeros((LANES, LANES), F32)
    for tap in range(TAPS):
        total = jnp.where(offset == tap, taps[tap].astype(F32), total)
    return total


def main_kernel(
    owner,
    delay,
    doppler,
    surv_taps,
    ref_taps,
    x_hbm,
    roots_hbm,
    out,
    x,
    roots,
    band,
    surv,
    picked,
    ref_in,
    gathered,
    reduced,
    refs,
    rows,
    corr_re,
    corr_im,
    table,
    outbox,
    in_x,
    in_z,
    sum_x,
    sum_z,
    last_x,
    last_z,
    sem_x,
    sem_roots,
    send_a,
    recv_a,
    send_b,
    recv_b,
    send_c,
    recv_c,
    send_d,
    recv_d,
):
    my_beam = lax.axis_index("beam")
    my_seg = lax.axis_index("seg")

    def fetch(c):
        at = pl.multiple_of(c * CHUNK, LANES)
        return pltpu.make_async_copy(
            x_hbm.at[:, :, pl.ds(at, CHUNK)],
            x.at[:, :, pl.ds(at + LANES, CHUNK)],
            sem_x.at[c],
        )

    for c in range(STEPS):
        fetch(c).start()
    fetch_roots = pltpu.make_async_copy(roots_hbm, roots, sem_roots)
    fetch_roots.start()

    barrier = pltpu.get_barrier_semaphore()
    for o in range(1, BEAM):
        peer = lax.rem(my_beam + o, BEAM)
        pl.semaphore_signal(barrier, inc=1, device_id={"beam": peer}, device_id_type=MESH)
    for o in range(1, SEG):
        peer = lax.rem(my_seg + o, SEG)
        pl.semaphore_signal(barrier, inc=1, device_id={"seg": peer}, device_id_type=MESH)

    wide = lax.broadcasted_iota(jnp.int32, (LANES, LANES), 1)
    forward = band_base(surv_taps, False)
    backward = band_base(ref_taps, True)
    for part in range(5):
        shift = 32 * (part - 1)
        ahead = pltpu.roll(forward, shift % LANES, axis=1)
        behind = pltpu.roll(backward, -shift % LANES, axis=1)
        if part == 0:
            ahead = jnp.where(wide < 8, ahead, 0.0)
            behind = jnp.where(wide >= LANES - 8, behind, 0.0)
        else:
            ahead = jnp.where(wide >= shift, ahead, 0.0)
            behind = jnp.where(wide < LANES - shift, behind, 0.0)
        band[part * LANES : (part + 1) * LANES, :LANES] = ahead.astype(BF16)
        band[part * LANES : (part + 1) * LANES, LANES:] = behind.astype(BF16)
    x[:, :, :LANES] = jnp.zeros((2, BEAMS_HERE, LANES), BF16)
    for r in range(4):
        picked[r * REGION + WINDOWS * 8 : (r + 1) * REGION, :] = jnp.zeros((64, LANES), F32)

    def decimate(step, _):
        fetch(step).wait()
        for group in range(WINDOWS_STEP // 8):
            pieces = []
            for w in range(8):
                q = step * WINDOWS_STEP + group * 8 + w
                at = pl.multiple_of(q * RAW_WINDOW, LANES)
                for part in range(2):
                    pieces.append(x[part, :, pl.ds(at, RAW_WINDOW + LANES)])
            left = jnp.concatenate(pieces, axis=0)
            both = jnp.dot(left, band[...], preferred_element_type=F32)
            for w in range(8):
                q = step * WINDOWS_STEP + group * 8 + w
                part_rows = both[w * 32 : (w + 1) * 32]
                surv[q] = part_rows[:, :LANES].astype(BF16)
                at = pl.multiple_of((WINDOWS - 1 - q) * 8, 8)
                for r in range(4):
                    picked[pl.ds(at + r * REGION, 8), :] = part_rows[8 * r : 8 * r + 8, LANES:]
        return 0

    lax.fori_loop(0, STEPS, decimate, 0)

    def pick(k):
        mine = lax.div(owner[k], BEAMS_HERE) == my_beam
        local = lax.rem(owner[k], BEAMS_HERE)
        whole = lax.div(delay[k], LANES)
        rest = lax.rem(delay[k], LANES)
        turn = lax.rem(LANES - rest, LANES)
        for part in range(2):
            start = (2 * part + lax.div(local, 8)) * REGION + whole * 8 + lax.rem(local, 8)
            first = picked[pl.ds(start, WINDOWS, stride=8), :]
            second = picked[pl.ds(start + 8, WINDOWS, stride=8), :]
            moved = jnp.where(
                wide < LANES - rest,
                pltpu.roll(first, turn, axis=1),
                pltpu.roll(second, turn, axis=1),
            )
            moved = jnp.where(mine, moved, 0.0).astype(BF16)
            ref_in[k, part * 8 : (part + 1) * 8] = moved.reshape(8, 16, LANES)

    groups = ((0, 1), (1, 3))

    def scatter(g, o):
        base, count = groups[g]
        peer = lax.rem(my_beam + o, BEAM)
        return pltpu.make_async_remote_copy(
            src_ref=ref_in.at[pl.ds(base, count), peer],
            dst_ref=gathered.at[o, pl.ds(base, count)],
            send_sem=send_a.at[g, o],
            recv_sem=recv_a.at[g, o],
            device_id={"beam": peer},
            device_id_type=MESH,
        )

    def spread(g, o):
        base, count = groups[g]
        peer = lax.rem(my_beam + o, BEAM)
        return pltpu.make_async_remote_copy(
            src_ref=reduced.at[pl.ds(base, count)],
            dst_ref=refs.at[pl.ds(base, count), my_beam],
            send_sem=send_b.at[g, o],
            recv_sem=recv_b.at[g, o],
            device_id={"beam": peer},
            device_id_type=MESH,
        )

    def spread_sums(g):
        base, count = groups[g]
        total = ref_in[base : base + count, my_beam].astype(F32)
        for o in range(1, BEAM):
            scatter(g, o).wait_recv()
            total = total + gathered[o, base : base + count].astype(F32)
        reduced[base : base + count] = total.astype(BF16)
        for o in range(1, BEAM):
            spread(g, o).start()
        refs[base : base + count, my_beam] = reduced[base : base + count]

    def arrive(g):
        base, count = groups[g]
        for o in range(1, BEAM):
            spread(g, o).wait_recv()
        for k in range(base, base + count):
            for part in range(2):
                flat = refs[k, part * 8 : (part + 1) * 8].reshape(WINDOWS, LANES)
                rows[2 * k + part, :WINDOWS] = flat.astype(F32)
                rows[2 * k + part, WINDOWS:] = jnp.zeros((8, LANES), F32)

    pick(0)
    pl.semaphore_wait(barrier, BEAM - 1 + SEG - 1)
    for o in range(1, BEAM):
        scatter(0, o).start()
    for k in range(1, TX):
        pick(k)
    for o in range(1, BEAM):
        scatter(1, o).start()
    fetch_roots.wait()
    spread_sums(0)
    spread_sums(1)
    arrive(0)

    lane = lax.broadcasted_iota(jnp.int32, (16, LANES), 1)
    sub = lax.broadcasted_iota(jnp.int32, (16, LANES), 0)
    low = lax.broadcasted_iota(jnp.int32, (32, LANES), 1) < BLOCK_LEN
    nil = jnp.zeros((32, LANES), BF16)

    my_z = lax.div(my_seg, 2)
    my_x = lax.rem(my_seg, 2)
    other = {"seg": 2 * my_z + 1 - my_x}

    def ring(dz):
        z = lax.rem(my_z + dz, 4)
        return z, {"seg": 2 * z + my_x}

    def remote(src, dst, send, recv, device):
        return pltpu.make_async_remote_copy(
            src_ref=src,
            dst_ref=dst,
            send_sem=send,
            recv_sem=recv,
            device_id=device,
            device_id_type=MESH,
        )

    def across(k):
        return remote(
            outbox.at[k, 0, :, 1 - my_x], in_x.at[k], send_c.at[k, 0], recv_c.at[k, 0], other
        )

    def around(k, dz):
        z, device = ring(dz)
        return remote(
            outbox.at[k, 1, z], in_z.at[k, dz], send_c.at[k, dz], recv_c.at[k, dz], device
        )

    def across_last(k):
        return remote(
            sum_z.at[k, 1 - my_x], last_x.at[k], send_d.at[k, 0], recv_d.at[k, 0], other
        )

    def around_last(k, dz):
        z, device = ring(dz)
        return remote(
            sum_x.at[k, z], last_z.at[k, dz], send_d.at[k, dz], recv_d.at[k, dz], device
        )

    def second(k):
        across(k).wait_recv()
        for z in range(4):
            total = outbox[k, 0, z, my_x].astype(F32) + in_x[k, z].astype(F32)
            sum_x[k, z] = total.astype(BF16)
        for dz in range(1, 4):
            around_last(k, dz).start()
        for dz in range(1, 4):
            around(k, dz).wait_recv()
        for side in range(2):
            total = outbox[k, 1, my_z, side].astype(F32)
            for dz in range(1, 4):
                total = total + in_z[k, dz, side].astype(F32)
            sum_z[k, side] = total.astype(BF16)
        across_last(k).start()

    def first(k, half):
        @pl.when(half == 0)
        def _():
            across(k).start()

        @pl.when(half == 1)
        def _():
            for dz in range(1, 4):
                around(k, dz).start()

    def staggered(kp, i):
        row = jnp.broadcast_to(rows[kp, pl.ds(i, 1), :], (8, LANES))
        top = pltpu.roll(row, 1, axis=1, stride=1, stride_axis=0)
        bottom = pltpu.roll(top, 8, axis=1)
        return jnp.concatenate([top, bottom], axis=0).astype(BF16)

    def toeplitz(below, above):
        tiles = []
        for c in range(8):
            mixed = jnp.where((lane < sub + 1) | (lane >= LANES - 16 * c), below, above)
            tiles.append(pltpu.roll(mixed, 16 * c, axis=1) if c else mixed)
        return jnp.concatenate(tiles, axis=0)

    def transmitter(k, _):
        def pair(step, _):
            stag = [
                [staggered(2 * k + part, WINDOWS - 2 * QUADS * step - r) for r in range(2 * QUADS + 1)]
                for part in range(2)
            ]
            for sub_q in range(QUADS):
                quad = QUADS * step + sub_q
                halves = []
                for a in range(2):
                    r = 2 * sub_q + a
                    halves.append(
                        jnp.concatenate(
                            [toeplitz(stag[part][r + 1], stag[part][r]) for part in range(2)],
                            axis=1,
                        )
                    )
                right = jnp.concatenate(halves, axis=0)
                s0 = surv[2 * quad]
                s1 = surv[2 * quad + 1]
                left = jnp.concatenate(
                    [
                        jnp.concatenate([jnp.where(low, s0, nil), nil], axis=1),
                        jnp.concatenate([jnp.where(low, nil, s0), nil], axis=1),
                        jnp.concatenate([nil, jnp.where(low, s1, nil)], axis=1),
                        jnp.concatenate([nil, jnp.where(low, nil, s1)], axis=1),
                    ],
                    axis=0,
                )
                prod = jnp.dot(left, right, preferred_element_type=F32)
                for l in range(4):
                    re = prod[32 * l : 32 * l + 16]
                    im = prod[32 * l + 16 : 32 * l + 32]
                    cre = re[:, :LANES] + im[:, LANES:]
                    cim = im[:, :LANES] - re[:, LANES:]
                    for half in range(2):
                        at = pl.multiple_of((4 * quad + l) * 8, 8) + half * 8 * BLOCKS
                        corr_re[pl.ds(at, 8), :] = cre[8 * half : 8 * half + 8]
                        corr_im[pl.ds(at, 8), :] = cim[8 * half : 8 * half + 8]
            return 0

        lax.fori_loop(0, WINDOWS // (2 * QUADS), pair, 0)

        for c in range(4):
            piece = roots[pl.ds(4 * doppler[k] + c, DOPPLER, stride=4), :].astype(BF16)
            table[:DOPPLER, c * LANES : (c + 1) * LANES] = piece
            if c < 2:
                table[DOPPLER:, BLOCKS + c * LANES : BLOCKS + (c + 1) * LANES] = piece
            else:
                table[DOPPLER:, (c - 2) * LANES : (c - 1) * LANES] = -piece

        def beams(half, _):
            def column(ref, b):
                at = half * 8 * BLOCKS + b
                return ref[pl.ds(at, BLOCKS, stride=8), :].astype(BF16)

            for bp in range(4):
                right = jnp.concatenate(
                    [
                        jnp.concatenate([column(ref, 2 * bp), column(ref, 2 * bp + 1)], axis=1)
                        for ref in (corr_re, corr_im)
                    ],
                    axis=0,
                )
                spec = jnp.dot(table[...], right, preferred_element_type=F32)
                sre, sim = spec[:DOPPLER], spec[DOPPLER:]
                power = (sre * sre + sim * sim) * (1.0 / (4 * BLOCKS * BLOCK_LEN))
                for b in range(2):
                    turned = power[:, b * LANES : (b + 1) * LANES].T.astype(BF16)
                    for g in range(SEG):
                        outbox[k, half, g // 2, g % 2, 2 * bp + b] = turned[16 * g : 16 * (g + 1)]
            first(k, half)
            return 0

        lax.fori_loop(0, 2, beams, 0)

        @pl.when(k == 0)
        def _():
            arrive(1)

        @pl.when(k > 0)
        def _():
            second(k - 1)

        return 0

    lax.fori_loop(0, TX, transmitter, 0)

    for g in range(2):
        for o in range(1, BEAM):
            scatter(g, o).wait_send()
            spread(g, o).wait_send()

    second(TX - 1)

    def collect(k, _):
        total = sum_x[k, my_z].astype(F32)
        for dz in range(1, 4):
            around_last(k, dz).wait_recv()
            total = total + last_z[k, dz].astype(F32)
        out[k, 0:8] = total * (1.0 / SEG)
        across_last(k).wait_recv()
        total = sum_z[k, my_x].astype(F32) + last_x[k].astype(F32)
        out[k, 8:16] = total * (1.0 / SEG)
        across(k).wait_send()
        across_last(k).wait_send()
        for dz in range(1, 4):
            around(k, dz).wait_send()
            around_last(k, dz).wait_send()
        return 0

    lax.fori_loop(0, TX, collect, 0)


def root_table():
    ells = np.arange(BLOCKS)[None, :]
    freqs = np.arange(2 * DOPPLER)[:, None] - BLOCKS // 2
    angle = 2.0 * np.pi / BLOCKS * ((ells * freqs) % BLOCKS)
    both = np.concatenate([np.cos(angle), np.sin(angle)], axis=1)
    return jnp.asarray(both.reshape(8 * DOPPLER, LANES), F32)


def shards(voltages, surv_taps, ref_taps, tx_owner, delay_start, doppler_start):
    smem = pl.BlockSpec(memory_space=pltpu.SMEM)
    hbm = pl.BlockSpec(memory_space=pl.ANY)
    dma = pltpu.SemaphoreType.DMA
    raw = DECIM * WINDOWS * LANES
    return pl.pallas_call(
        main_kernel,
        in_specs=[smem] * 5 + [hbm] * 2,
        out_specs=pl.BlockSpec(memory_space=pltpu.VMEM),
        out_shape=jax.ShapeDtypeStruct((TX, BEAMS_HERE, DELAYS // SEG, DOPPLER), F32),
        scratch_shapes=[
            pltpu.VMEM((2, BEAMS_HERE, raw + LANES), BF16),
            pltpu.VMEM((8 * DOPPLER, LANES), F32),
            pltpu.VMEM((5 * LANES, 2 * LANES), BF16),
            pltpu.VMEM((WINDOWS, 32, LANES), BF16),
            pltpu.VMEM((4 * REGION, LANES), F32),
            pltpu.VMEM((TX, BEAM, 16, LANES), BF16),
            pltpu.VMEM((BEAM, TX, 16, LANES), BF16),
            pltpu.VMEM((TX, 16, LANES), BF16),
            pltpu.VMEM((TX, BEAM, 16, LANES), BF16),
            pltpu.VMEM((2 * TX, WINDOWS + 8, LANES), F32),
            pltpu.VMEM((BEAMS_HERE * BLOCKS, LANES), F32),
            pltpu.VMEM((BEAMS_HERE * BLOCKS, LANES), F32),
            pltpu.VMEM((2 * DOPPLER, 2 * BLOCKS), BF16),
            pltpu.VMEM((TX, 2, 4, 2, 8, 16, LANES), BF16),
            pltpu.VMEM((TX, 4, 8, 16, LANES), BF16),
            pltpu.VMEM((TX, 4, 2, 8, 16, LANES), BF16),
            pltpu.VMEM((TX, 4, 8, 16, LANES), BF16),
            pltpu.VMEM((TX, 2, 8, 16, LANES), BF16),
            pltpu.VMEM((TX, 8, 16, LANES), BF16),
            pltpu.VMEM((TX, 4, 8, 16, LANES), BF16),
            dma((STEPS,)),
            dma,
            dma((2, BEAM)),
            dma((2, BEAM)),
            dma((2, BEAM)),
            dma((2, BEAM)),
            dma((TX, 4)),
            dma((TX, 4)),
            dma((TX, 4)),
            dma((TX, 4)),
        ],
        compiler_params=pltpu.CompilerParams(collective_id=0, has_side_effects=True),
        name="ambiguity",
    )(
        tx_owner,
        delay_start,
        doppler_start,
        surv_taps,
        ref_taps,
        voltages.reshape(2, BEAMS_HERE, raw),
        root_table(),
    )


def solution(mesh):
    return jax.shard_map(
        shards,
        mesh=mesh,
        in_specs=(P(None, "beam", "seg", None), P(), P(), P(), P(), P()),
        out_specs=P(None, "beam", "seg", None),
        check_vma=False,
    )
```

```python
import functools

import jax
import jax.numpy as jnp
import numpy as np
from jax import lax
from jax.experimental import pallas as pl
from jax.experimental.pallas import tpu as pltpu
from jax.sharding import PartitionSpec as P

TX = 4
DECIM = 4
TAPS = 32
BLOCK_LEN = 64
BLOCKS = 256
DELAYS = 128
DOPPLER = 128
LANES = 128
BEAMS_HERE = 16
WINDOWS = 128
WINDOWS_STEP = 32
CHUNK = WINDOWS_STEP * 512
STEPS = WINDOWS // WINDOWS_STEP
RAW_WINDOW = DECIM * LANES
REGION = (WINDOWS + 8) * 8
BEAM = 16
SEG = 8
QUADS = 64
F32 = jnp.float32
BF16 = jnp.bfloat16
MESH = pl.DeviceIdType.MESH


def band_base(taps, backwards):
    rows = lax.broadcasted_iota(jnp.int32, (LANES, LANES), 0)
    cols = lax.broadcasted_iota(jnp.int32, (LANES, LANES), 1)
    if backwards:
        cols = LANES - 1 - cols
    offset = DECIM * cols - rows
    total = jnp.zeros((LANES, LANES), F32)
    for tap in range(TAPS):
        total = jnp.where(offset == tap, taps[tap].astype(F32), total)
    return total


def main_kernel(
    owner,
    delay,
    doppler,
    surv_taps,
    ref_taps,
    x_hbm,
    roots_hbm,
    out,
    x,
    roots,
    band,
    surv,
    picked,
    ref_in,
    gathered,
    reduced,
    refs,
    rows,
    leaning,
    corr_re,
    corr_im,
    table,
    outbox,
    in_x,
    in_z,
    sum_x,
    sum_z,
    last_x,
    last_z,
    inbox,
    sem_x,
    sem_roots,
    send_a,
    recv_a,
    send_b,
    recv_b,
    send_c,
    recv_c,
    send_d,
    recv_d,
    send_e,
    recv_e,
):
    my_beam = lax.axis_index("beam")
    my_seg = lax.axis_index("seg")

    def fetch(c):
        at = pl.multiple_of(c * CHUNK, LANES)
        return pltpu.make_async_copy(
            x_hbm.at[:, :, pl.ds(at, CHUNK)],
            x.at[:, :, pl.ds(at + LANES, CHUNK)],
            sem_x.at[c],
        )

    for c in range(STEPS):
        fetch(c).start()
    fetch_roots = pltpu.make_async_copy(roots_hbm, roots, sem_roots)
    fetch_roots.start()

    barrier = pltpu.get_barrier_semaphore()
    for o in range(1, BEAM):
        peer = lax.rem(my_beam + o, BEAM)
        pl.semaphore_signal(barrier, inc=1, device_id={"beam": peer}, device_id_type=MESH)
    for o in range(1, SEG):
        peer = lax.rem(my_seg + o, SEG)
        pl.semaphore_signal(barrier, inc=1, device_id={"seg": peer}, device_id_type=MESH)

    wide = lax.broadcasted_iota(jnp.int32, (LANES, LANES), 1)
    forward = band_base(surv_taps, False)
    backward = band_base(ref_taps, True)
    for part in range(5):
        shift = 32 * (part - 1)
        ahead = pltpu.roll(forward, shift % LANES, axis=1)
        behind = pltpu.roll(backward, -shift % LANES, axis=1)
        if part == 0:
            ahead = jnp.where(wide < 8, ahead, 0.0)
            behind = jnp.where(wide >= LANES - 8, behind, 0.0)
        else:
            ahead = jnp.where(wide >= shift, ahead, 0.0)
            behind = jnp.where(wide < LANES - shift, behind, 0.0)
        band[part * LANES : (part + 1) * LANES, :LANES] = ahead.astype(BF16)
        band[part * LANES : (part + 1) * LANES, LANES:] = behind.astype(BF16)
    x[:, :, :LANES] = jnp.zeros((2, BEAMS_HERE, LANES), BF16)
    for r in range(4):
        picked[r * REGION + WINDOWS * 8 : (r + 1) * REGION, :] = jnp.zeros((64, LANES), F32)

    def decimate(step, _):
        fetch(step).wait()
        for group in range(WINDOWS_STEP // 8):
            pieces = []
            for w in range(8):
                q = step * WINDOWS_STEP + group * 8 + w
                at = pl.multiple_of(q * RAW_WINDOW, LANES)
                for part in range(2):
                    pieces.append(x[part, :, pl.ds(at, RAW_WINDOW + LANES)])
            left = jnp.concatenate(pieces, axis=0)
            both = jnp.dot(left, band[...], preferred_element_type=F32)
            for w in range(8):
                q = step * WINDOWS_STEP + group * 8 + w
                part_rows = both[w * 32 : (w + 1) * 32]
                surv[q] = part_rows[:, :LANES].astype(BF16)
                at = pl.multiple_of((WINDOWS - 1 - q) * 8, 8)
                for r in range(4):
                    picked[pl.ds(at + r * REGION, 8), :] = part_rows[8 * r : 8 * r + 8, LANES:]
        return 0

    lax.fori_loop(0, STEPS, decimate, 0)

    def pick(k):
        mine = lax.div(owner[k], BEAMS_HERE) == my_beam
        local = lax.rem(owner[k], BEAMS_HERE)
        whole = lax.div(delay[k], LANES)
        rest = lax.rem(delay[k], LANES)
        turn = lax.rem(LANES - rest, LANES)
        for part in range(2):
            start = (2 * part + lax.div(local, 8)) * REGION + whole * 8 + lax.rem(local, 8)
            first = picked[pl.ds(start, WINDOWS, stride=8), :]
            second = picked[pl.ds(start + 8, WINDOWS, stride=8), :]
            moved = jnp.where(
                wide < LANES - rest,
                pltpu.roll(first, turn, axis=1),
                pltpu.roll(second, turn, axis=1),
            )
            moved = jnp.where(mine, moved, 0.0).astype(BF16)
            ref_in[k, part * 8 : (part + 1) * 8] = moved.reshape(8, 16, LANES)

    groups = ((0, 1), (1, 3))

    def scatter(g, o):
        base, count = groups[g]
        peer = lax.rem(my_beam + o, BEAM)
        return pltpu.make_async_remote_copy(
            src_ref=ref_in.at[pl.ds(base, count), peer],
            dst_ref=gathered.at[o, pl.ds(base, count)],
            send_sem=send_a.at[g, o],
            recv_sem=recv_a.at[g, o],
            device_id={"beam": peer},
            device_id_type=MESH,
        )

    def spread(g, o):
        base, count = groups[g]
        peer = lax.rem(my_beam + o, BEAM)
        return pltpu.make_async_remote_copy(
            src_ref=reduced.at[pl.ds(base, count)],
            dst_ref=refs.at[pl.ds(base, count), my_beam],
            send_sem=send_b.at[g, o],
            recv_sem=recv_b.at[g, o],
            device_id={"beam": peer},
            device_id_type=MESH,
        )

    def spread_sums(g):
        base, count = groups[g]
        total = ref_in[base : base + count, my_beam].astype(F32)
        for o in range(1, BEAM):
            scatter(g, o).wait_recv()
            total = total + gathered[o, base : base + count].astype(F32)
        reduced[base : base + count] = total.astype(BF16)
        for o in range(1, BEAM):
            spread(g, o).start()
        refs[base : base + count, my_beam] = reduced[base : base + count]

    def arrive(g):
        base, count = groups[g]
        for o in range(1, BEAM):
            spread(g, o).wait_recv()
        for k in range(base, base + count):
            for part in range(2):
                flat = refs[k, part * 8 : (part + 1) * 8].reshape(WINDOWS, LANES)
                rows[2 * k + part, :WINDOWS] = flat.astype(F32)

        def stagger(step, _):
            for r in range(64):
                kp = 2 * base + lax.div(step, 2)
                i = lax.rem(step, 2) * 64 + r
                row = jnp.broadcast_to(rows[kp, pl.ds(i, 1), :], (8, LANES))
                top = pltpu.roll(row, 1, axis=1, stride=1, stride_axis=0)
                bottom = pltpu.roll(row, 9, axis=1, stride=1, stride_axis=0)
                leaning[kp, i] = jnp.concatenate([top, bottom], axis=0).astype(BF16)
            return 0

        lax.fori_loop(0, 4 * count, stagger, 0)

    pick(0)
    pl.semaphore_wait(barrier, BEAM - 1 + SEG - 1)
    for o in range(1, BEAM):
        scatter(0, o).start()
    for k in range(1, TX):
        pick(k)
    for o in range(1, BEAM):
        scatter(1, o).start()
    fetch_roots.wait()
    spread_sums(0)
    spread_sums(1)
    arrive(0)

    lane = lax.broadcasted_iota(jnp.int32, (16, LANES), 1)
    sub = lax.broadcasted_iota(jnp.int32, (16, LANES), 0)
    low = lax.broadcasted_iota(jnp.int32, (32, LANES), 1) < BLOCK_LEN
    nil = jnp.zeros((32, LANES), BF16)

    my_z = lax.div(my_seg, 2)
    my_x = lax.rem(my_seg, 2)
    other = {"seg": 2 * my_z + 1 - my_x}

    def ring(dz):
        z = lax.rem(my_z + dz, 4)
        return z, {"seg": 2 * z + my_x}

    def remote(src, dst, send, recv, device):
        return pltpu.make_async_remote_copy(
            src_ref=src,
            dst_ref=dst,
            send_sem=send,
            recv_sem=recv,
            device_id=device,
            device_id_type=MESH,
        )

    def across(k):
        return remote(
            outbox.at[k, 0, :, 1 - my_x], in_x.at[k], send_c.at[k, 0], recv_c.at[k, 0], other
        )

    def around(k, dz):
        z, device = ring(dz)
        return remote(
            outbox.at[k, 1, z], in_z.at[k, dz], send_c.at[k, dz], recv_c.at[k, dz], device
        )

    def across_last(k):
        return remote(
            sum_z.at[k, 1 - my_x], last_x.at[k], send_d.at[k, 0], recv_d.at[k, 0], other
        )

    def around_last(k, dz):
        z, device = ring(dz)
        return remote(
            sum_x.at[k, z], last_z.at[k, dz], send_d.at[k, dz], recv_d.at[k, dz], device
        )

    def second(k):
        across(k).wait_recv()
        for z in range(4):
            total = outbox[k, 0, z, my_x].astype(F32) + in_x[k, z].astype(F32)
            sum_x[k, z] = total.astype(BF16)
        for dz in range(1, 4):
            around_last(k, dz).start()
        for dz in range(1, 4):
            around(k, dz).wait_recv()
        for side in range(2):
            total = outbox[k, 1, my_z, side].astype(F32)
            for dz in range(1, 4):
                total = total + in_z[k, dz, side].astype(F32)
            sum_z[k, side] = total.astype(BF16)
        across_last(k).start()

    def straight(half, o):
        peer = lax.rem(my_seg + o, SEG)
        return remote(
            outbox.at[TX - 1, half, lax.div(peer, 2), lax.rem(peer, 2)],
            inbox.at[half, o],
            send_e.at[half, o],
            recv_e.at[half, o],
            {"seg": peer},
        )

    def first(k, half):
        @pl.when((half == 0) & (k < TX - 1))
        def _():
            across(k).start()

        @pl.when((half == 1) & (k < TX - 1))
        def _():
            for dz in range(1, 4):
                around(k, dz).start()

        @pl.when(k == TX - 1)
        def _():
            for o in range(1, SEG):
                straight(half, o).start()

    for kp in range(2 * TX):
        leaning[kp, WINDOWS] = jnp.zeros((16, LANES), BF16)

    def staggered(kp, i):
        return leaning[kp, i]

    def turns(u):
        return [u] + [pltpu.roll(u, 16 * c, axis=1) for c in range(1, 4)]

    def toeplitz(below, above):
        even, odd = [], []
        for c in range(4):
            near = lane < sub + 1 + 16 * c
            even.append(jnp.where(near, below[c], above[c]))
            odd.append(jnp.where(near | (lane >= BLOCK_LEN), below[c], above[c]))
        return jnp.concatenate(even + odd, axis=0)

    def transmitter(k, _):
        def pair(step, _):
            def row_of(r):
                return [turns(staggered(2 * k + part, WINDOWS - 2 * QUADS * step - r)) for part in range(2)]

            above = row_of(0)
            for sub_q in range(QUADS):
                quad = QUADS * step + sub_q
                halves = []
                for a in range(2):
                    r = 2 * sub_q + a
                    below = row_of(r + 1)
                    halves.append(
                        jnp.concatenate(
                            [toeplitz(below[part], above[part]) for part in range(2)], axis=1
                        )
                    )
                    above = below
                right = jnp.concatenate(halves, axis=0)
                s0 = surv[2 * quad]
                s1 = surv[2 * quad + 1]
                left = jnp.concatenate(
                    [
                        jnp.concatenate([jnp.where(low, s0, nil), nil], axis=1),
                        jnp.concatenate([jnp.where(low, nil, s0), nil], axis=1),
                        jnp.concatenate([nil, jnp.where(low, s1, nil)], axis=1),
                        jnp.concatenate([nil, jnp.where(low, nil, s1)], axis=1),
                    ],
                    axis=0,
                )
                prod = jnp.dot(left, right, preferred_element_type=F32)
                for l in range(4):
                    re = prod[32 * l : 32 * l + 16]
                    im = prod[32 * l + 16 : 32 * l + 32]
                    cre = re[:, :LANES] + im[:, LANES:]
                    cim = im[:, :LANES] - re[:, LANES:]
                    for half in range(2):
                        at = pl.multiple_of((2 * quad + l // 2) * 8, 8) + (l % 2) * 4 * BLOCKS
                        at = at + half * 8 * BLOCKS
                        corr_re[pl.ds(at, 8), :] = cre[8 * half : 8 * half + 8]
                        corr_im[pl.ds(at, 8), :] = cim[8 * half : 8 * half + 8]
            return 0

        lax.fori_loop(0, WINDOWS // (2 * QUADS), pair, 0)

        for c in range(4):
            piece = roots[pl.ds(4 * doppler[k] + c, DOPPLER, stride=4), :].astype(BF16)
            table[:DOPPLER, c * LANES : (c + 1) * LANES] = piece
            if c < 2:
                table[DOPPLER:, BLOCKS + c * LANES : BLOCKS + (c + 1) * LANES] = piece
            else:
                table[DOPPLER:, (c - 2) * LANES : (c - 1) * LANES] = -piece

        def beams(half, _):
            def column(ref, b):
                at = half * 8 * BLOCKS + b
                even = ref[pl.ds(at, LANES, stride=8), :].astype(BF16)
                odd = ref[pl.ds(at + 8 * LANES, LANES, stride=8), :].astype(BF16)
                return jnp.concatenate([even, pltpu.roll(odd, BLOCK_LEN, axis=1)], axis=0)

            for bp in range(4):
                right = jnp.concatenate(
                    [
                        jnp.concatenate([column(ref, 2 * bp), column(ref, 2 * bp + 1)], axis=1)
                        for ref in (corr_re, corr_im)
                    ],
                    axis=0,
                )
                spec = jnp.dot(table[...], right, preferred_element_type=F32)
                sre, sim = spec[:DOPPLER], spec[DOPPLER:]
                power = (sre * sre + sim * sim) * (1.0 / (4 * BLOCKS * BLOCK_LEN))
                for b in range(2):
                    turned = power[:, b * LANES : (b + 1) * LANES].T.astype(BF16)
                    for g in range(SEG):
                        outbox[k, half, g // 2, g % 2, 2 * bp + b] = turned[16 * g : 16 * (g + 1)]
            first(k, half)
            return 0

        lax.fori_loop(0, 2, beams, 0)

        @pl.when(k == 0)
        def _():
            arrive(1)

        @pl.when(k > 0)
        def _():
            second(k - 1)

        return 0

    lax.fori_loop(0, TX, transmitter, 0)

    for g in range(2):
        for o in range(1, BEAM):
            scatter(g, o).wait_send()
            spread(g, o).wait_send()

    def collect(k, _):
        total = sum_x[k, my_z].astype(F32)
        for dz in range(1, 4):
            around_last(k, dz).wait_recv()
            total = total + last_z[k, dz].astype(F32)
        out[k, 0:8] = total * (1.0 / SEG)
        across_last(k).wait_recv()
        total = sum_z[k, my_x].astype(F32) + last_x[k].astype(F32)
        out[k, 8:16] = total * (1.0 / SEG)
        across(k).wait_send()
        across_last(k).wait_send()
        for dz in range(1, 4):
            around(k, dz).wait_send()
            around_last(k, dz).wait_send()
        return 0

    lax.fori_loop(0, TX - 1, collect, 0)

    for half in range(2):
        total = outbox[TX - 1, half, my_z, my_x].astype(F32)
        for o in range(1, SEG):
            straight(half, o).wait_recv()
            total = total + inbox[half, o].astype(F32)
        out[TX - 1, 8 * half : 8 * half + 8] = total * (1.0 / SEG)
    for half in range(2):
        for o in range(1, SEG):
            straight(half, o).wait_send()


def root_table():
    ells = np.arange(BLOCKS).reshape(LANES, 2).T.reshape(1, BLOCKS)
    freqs = np.arange(2 * DOPPLER)[:, None] - BLOCKS // 2
    angle = 2.0 * np.pi / BLOCKS * ((ells * freqs) % BLOCKS)
    both = np.concatenate([np.cos(angle), np.sin(angle)], axis=1)
    return jnp.asarray(both.reshape(8 * DOPPLER, LANES), F32)


def shards(voltages, surv_taps, ref_taps, tx_owner, delay_start, doppler_start):
    smem = pl.BlockSpec(memory_space=pltpu.SMEM)
    hbm = pl.BlockSpec(memory_space=pl.ANY)
    dma = pltpu.SemaphoreType.DMA
    raw = DECIM * WINDOWS * LANES
    return pl.pallas_call(
        main_kernel,
        in_specs=[smem] * 5 + [hbm] * 2,
        out_specs=pl.BlockSpec(memory_space=pltpu.VMEM),
        out_shape=jax.ShapeDtypeStruct((TX, BEAMS_HERE, DELAYS // SEG, DOPPLER), F32),
        scratch_shapes=[
            pltpu.VMEM((2, BEAMS_HERE, raw + LANES), BF16),
            pltpu.VMEM((8 * DOPPLER, LANES), F32),
            pltpu.VMEM((5 * LANES, 2 * LANES), BF16),
            pltpu.VMEM((WINDOWS, 32, LANES), BF16),
            pltpu.VMEM((4 * REGION, LANES), F32),
            pltpu.VMEM((TX, BEAM, 16, LANES), BF16),
            pltpu.VMEM((BEAM, TX, 16, LANES), BF16),
            pltpu.VMEM((TX, 16, LANES), BF16),
            pltpu.VMEM((TX, BEAM, 16, LANES), BF16),
            pltpu.VMEM((2 * TX, WINDOWS, LANES), F32),
            pltpu.VMEM((2 * TX, WINDOWS + 1, 16, LANES), BF16),
            pltpu.VMEM((BEAMS_HERE * BLOCKS, LANES), F32),
            pltpu.VMEM((BEAMS_HERE * BLOCKS, LANES), F32),
            pltpu.VMEM((2 * DOPPLER, 2 * BLOCKS), BF16),
            pltpu.VMEM((TX, 2, 4, 2, 8, 16, LANES), BF16),
            pltpu.VMEM((TX, 4, 8, 16, LANES), BF16),
            pltpu.VMEM((TX, 4, 2, 8, 16, LANES), BF16),
            pltpu.VMEM((TX, 4, 8, 16, LANES), BF16),
            pltpu.VMEM((TX, 2, 8, 16, LANES), BF16),
            pltpu.VMEM((TX, 8, 16, LANES), BF16),
            pltpu.VMEM((TX, 4, 8, 16, LANES), BF16),
            pltpu.VMEM((2, SEG, 8, 16, LANES), BF16),
            dma((STEPS,)),
            dma,
            dma((2, BEAM)),
            dma((2, BEAM)),
            dma((2, BEAM)),
            dma((2, BEAM)),
            dma((TX, 4)),
            dma((TX, 4)),
            dma((TX, 4)),
            dma((TX, 4)),
            dma((2, SEG)),
            dma((2, SEG)),
        ],
        compiler_params=pltpu.CompilerParams(collective_id=0, has_side_effects=True),
        name="ambiguity",
    )(
        tx_owner,
        delay_start,
        doppler_start,
        surv_taps,
        ref_taps,
        voltages.reshape(2, BEAMS_HERE, raw),
        root_table(),
    )


def solution(mesh):
    return jax.shard_map(
        shards,
        mesh=mesh,
        in_specs=(P(None, "beam", "seg", None), P(), P(), P(), P(), P()),
        out_specs=P(None, "beam", "seg", None),
        check_vma=False,
    )
```

```python
import functools

import jax
import jax.numpy as jnp
import numpy as np
from jax import lax
from jax.experimental import pallas as pl
from jax.experimental.pallas import tpu as pltpu
from jax.sharding import PartitionSpec as P

TX = 4
DECIM = 4
TAPS = 32
BLOCK_LEN = 64
BLOCKS = 256
DELAYS = 128
DOPPLER = 128
LANES = 128
BEAMS_HERE = 16
WINDOWS = 128
WINDOWS_STEP = 32
CHUNK = WINDOWS_STEP * 512
STEPS = WINDOWS // WINDOWS_STEP
RAW_WINDOW = DECIM * LANES
REGION = (WINDOWS + 8) * 8
BEAM = 16
SEG = 8
QUADS = 64
F32 = jnp.float32
BF16 = jnp.bfloat16
MESH = pl.DeviceIdType.MESH


def band_base(taps, backwards):
    rows = lax.broadcasted_iota(jnp.int32, (LANES, LANES), 0)
    cols = lax.broadcasted_iota(jnp.int32, (LANES, LANES), 1)
    if backwards:
        cols = LANES - 1 - cols
    offset = DECIM * cols - rows
    total = jnp.zeros((LANES, LANES), F32)
    for tap in range(TAPS):
        total = jnp.where(offset == tap, taps[tap].astype(F32), total)
    return total


def main_kernel(
    owner,
    delay,
    doppler,
    surv_taps,
    ref_taps,
    x_hbm,
    roots_hbm,
    out,
    x,
    roots,
    band,
    surv,
    picked,
    ref_in,
    gathered,
    reduced,
    refs,
    rows,
    leaning,
    corr_re,
    corr_im,
    table,
    outbox,
    in_x,
    in_z,
    sum_x,
    sum_z,
    last_x,
    last_z,
    inbox,
    sem_x,
    sem_roots,
    send_a,
    recv_a,
    send_b,
    recv_b,
    send_c,
    recv_c,
    send_d,
    recv_d,
    send_e,
    recv_e,
):
    my_beam = lax.axis_index("beam")
    my_seg = lax.axis_index("seg")

    def fetch(c):
        at = pl.multiple_of(c * CHUNK, LANES)
        return pltpu.make_async_copy(
            x_hbm.at[:, :, pl.ds(at, CHUNK)],
            x.at[:, :, pl.ds(at + LANES, CHUNK)],
            sem_x.at[c],
        )

    for c in range(STEPS):
        fetch(c).start()
    fetch_roots = pltpu.make_async_copy(roots_hbm, roots, sem_roots)
    fetch_roots.start()

    barrier = pltpu.get_barrier_semaphore()
    for o in range(1, BEAM):
        peer = lax.rem(my_beam + o, BEAM)
        pl.semaphore_signal(barrier, inc=1, device_id={"beam": peer}, device_id_type=MESH)
    for o in range(1, SEG):
        peer = lax.rem(my_seg + o, SEG)
        pl.semaphore_signal(barrier, inc=1, device_id={"seg": peer}, device_id_type=MESH)

    wide = lax.broadcasted_iota(jnp.int32, (LANES, LANES), 1)
    forward = band_base(surv_taps, False)
    backward = band_base(ref_taps, True)
    for part in range(5):
        shift = 32 * (part - 1)
        ahead = pltpu.roll(forward, shift % LANES, axis=1)
        behind = pltpu.roll(backward, -shift % LANES, axis=1)
        if part == 0:
            ahead = jnp.where(wide < 8, ahead, 0.0)
            behind = jnp.where(wide >= LANES - 8, behind, 0.0)
        else:
            ahead = jnp.where(wide >= shift, ahead, 0.0)
            behind = jnp.where(wide < LANES - shift, behind, 0.0)
        band[part * LANES : (part + 1) * LANES, :LANES] = ahead.astype(BF16)
        band[part * LANES : (part + 1) * LANES, LANES:] = behind.astype(BF16)
    x[:, :, :LANES] = jnp.zeros((2, BEAMS_HERE, LANES), BF16)
    for r in range(4):
        picked[r * REGION + WINDOWS * 8 : (r + 1) * REGION, :] = jnp.zeros((64, LANES), F32)

    def decimate(step, _):
        fetch(step).wait()
        for group in range(WINDOWS_STEP // 8):
            pieces = []
            for w in range(8):
                q = step * WINDOWS_STEP + group * 8 + w
                at = pl.multiple_of(q * RAW_WINDOW, LANES)
                for part in range(2):
                    pieces.append(x[part, :, pl.ds(at, RAW_WINDOW + LANES)])
            left = jnp.concatenate(pieces, axis=0)
            both = jnp.dot(left, band[...], preferred_element_type=F32)
            for w in range(8):
                q = step * WINDOWS_STEP + group * 8 + w
                part_rows = both[w * 32 : (w + 1) * 32]
                surv[q] = part_rows[:, :LANES].astype(BF16)
                at = pl.multiple_of((WINDOWS - 1 - q) * 8, 8)
                for r in range(4):
                    picked[pl.ds(at + r * REGION, 8), :] = part_rows[8 * r : 8 * r + 8, LANES:]
        return 0

    lax.fori_loop(0, STEPS, decimate, 0)

    def pick(k):
        mine = lax.div(owner[k], BEAMS_HERE) == my_beam
        local = lax.rem(owner[k], BEAMS_HERE)
        whole = lax.div(delay[k], LANES)
        rest = lax.rem(delay[k], LANES)
        turn = lax.rem(LANES - rest, LANES)
        for part in range(2):
            start = (2 * part + lax.div(local, 8)) * REGION + whole * 8 + lax.rem(local, 8)
            first = picked[pl.ds(start, WINDOWS, stride=8), :]
            second = picked[pl.ds(start + 8, WINDOWS, stride=8), :]
            moved = jnp.where(
                wide < LANES - rest,
                pltpu.roll(first, turn, axis=1),
                pltpu.roll(second, turn, axis=1),
            )
            moved = jnp.where(mine, moved, 0.0).astype(BF16)
            ref_in[k, part * 8 : (part + 1) * 8] = moved.reshape(8, 16, LANES)

    groups = ((0, 1), (1, 3))

    def scatter(g, o):
        base, count = groups[g]
        peer = lax.rem(my_beam + o, BEAM)
        return pltpu.make_async_remote_copy(
            src_ref=ref_in.at[pl.ds(base, count), peer],
            dst_ref=gathered.at[o, pl.ds(base, count)],
            send_sem=send_a.at[g, o],
            recv_sem=recv_a.at[g, o],
            device_id={"beam": peer},
            device_id_type=MESH,
        )

    def spread(g, o):
        base, count = groups[g]
        peer = lax.rem(my_beam + o, BEAM)
        return pltpu.make_async_remote_copy(
            src_ref=reduced.at[pl.ds(base, count)],
            dst_ref=refs.at[pl.ds(base, count), my_beam],
            send_sem=send_b.at[g, o],
            recv_sem=recv_b.at[g, o],
            device_id={"beam": peer},
            device_id_type=MESH,
        )

    def spread_sums(g):
        base, count = groups[g]
        total = ref_in[base : base + count, my_beam].astype(F32)
        for o in range(1, BEAM):
            scatter(g, o).wait_recv()
            total = total + gathered[o, base : base + count].astype(F32)
        reduced[base : base + count] = total.astype(BF16)
        for o in range(1, BEAM):
            spread(g, o).start()
        refs[base : base + count, my_beam] = reduced[base : base + count]

    def arrive(g):
        base, count = groups[g]
        for o in range(1, BEAM):
            spread(g, o).wait_recv()
        for k in range(base, base + count):
            for part in range(2):
                flat = refs[k, part * 8 : (part + 1) * 8].reshape(WINDOWS, LANES)
                rows[2 * k + part, :WINDOWS] = flat.astype(F32)

        def stagger(step, _):
            for r in range(64):
                kp = 2 * base + lax.div(step, 2)
                i = lax.rem(step, 2) * 64 + r
                row = jnp.broadcast_to(rows[kp, pl.ds(i, 1), :], (8, LANES))
                top = pltpu.roll(row, 1, axis=1, stride=1, stride_axis=0)
                bottom = pltpu.roll(row, 9, axis=1, stride=1, stride_axis=0)
                leaning[kp, i] = jnp.concatenate([top, bottom], axis=0).astype(BF16)
            return 0

        lax.fori_loop(0, 4 * count, stagger, 0)

    pick(0)
    pl.semaphore_wait(barrier, BEAM - 1 + SEG - 1)
    for o in range(1, BEAM):
        scatter(0, o).start()
    for k in range(1, TX):
        pick(k)
    for o in range(1, BEAM):
        scatter(1, o).start()
    fetch_roots.wait()
    spread_sums(0)
    spread_sums(1)
    arrive(0)

    lane = lax.broadcasted_iota(jnp.int32, (16, LANES), 1)
    sub = lax.broadcasted_iota(jnp.int32, (16, LANES), 0)
    low = lax.broadcasted_iota(jnp.int32, (32, LANES), 1) < BLOCK_LEN
    nil = jnp.zeros((32, LANES), BF16)

    my_z = lax.div(my_seg, 2)
    my_x = lax.rem(my_seg, 2)
    other = {"seg": 2 * my_z + 1 - my_x}

    def ring(dz):
        z = lax.rem(my_z + dz, 4)
        return z, {"seg": 2 * z + my_x}

    def remote(src, dst, send, recv, device):
        return pltpu.make_async_remote_copy(
            src_ref=src,
            dst_ref=dst,
            send_sem=send,
            recv_sem=recv,
            device_id=device,
            device_id_type=MESH,
        )

    def across(k):
        return remote(
            outbox.at[k, 0, :, 1 - my_x], in_x.at[k], send_c.at[k, 0], recv_c.at[k, 0], other
        )

    def around(k, dz):
        z, device = ring(dz)
        return remote(
            outbox.at[k, 1, z], in_z.at[k, dz], send_c.at[k, dz], recv_c.at[k, dz], device
        )

    def across_last(k):
        return remote(
            sum_z.at[k, 1 - my_x], last_x.at[k], send_d.at[k, 0], recv_d.at[k, 0], other
        )

    def around_last(k, dz):
        z, device = ring(dz)
        return remote(
            sum_x.at[k, z], last_z.at[k, dz], send_d.at[k, dz], recv_d.at[k, dz], device
        )

    def second(k):
        for dz in range(1, 4):
            around(k, dz).wait_recv()
        for side in range(2):
            total = outbox[k, 1, my_z, side].astype(F32)
            for dz in range(1, 4):
                total = total + in_z[k, dz, side].astype(F32)
            sum_z[k, side] = total.astype(BF16)
        across_last(k).start()
        across(k).wait_recv()
        for z in range(4):
            total = outbox[k, 0, z, my_x].astype(F32) + in_x[k, z].astype(F32)
            sum_x[k, z] = total.astype(BF16)
        for dz in range(1, 4):
            around_last(k, dz).start()

    def straight(half, o):
        peer = lax.rem(my_seg + o, SEG)
        return remote(
            outbox.at[TX - 1, half, lax.div(peer, 2), lax.rem(peer, 2)],
            inbox.at[half, o],
            send_e.at[half, o],
            recv_e.at[half, o],
            {"seg": peer},
        )

    def first(k, half):
        @pl.when((half == 0) & (k < TX - 1))
        def _():
            across(k).start()

        @pl.when((half == 1) & (k < TX - 1))
        def _():
            for dz in range(1, 4):
                around(k, dz).start()

        @pl.when(k == TX - 1)
        def _():
            for o in range(1, SEG):
                straight(half, o).start()

    for kp in range(2 * TX):
        leaning[kp, WINDOWS] = jnp.zeros((16, LANES), BF16)

    def staggered(kp, i):
        return leaning[kp, i]

    def turns(u):
        return [u] + [pltpu.roll(u, 16 * c, axis=1) for c in range(1, 4)]

    def toeplitz(below, above):
        even, odd = [], []
        for c in range(4):
            near = lane < sub + 1 + 16 * c
            even.append(jnp.where(near, below[c], above[c]))
            odd.append(jnp.where(near | (lane >= BLOCK_LEN), below[c], above[c]))
        return jnp.concatenate(even + odd, axis=0)

    def transmitter(k, _):
        def pair(step, _):
            def row_of(r):
                return [turns(staggered(2 * k + part, WINDOWS - 2 * QUADS * step - r)) for part in range(2)]

            above = row_of(0)
            for sub_q in range(QUADS):
                quad = QUADS * step + sub_q
                halves = []
                for a in range(2):
                    r = 2 * sub_q + a
                    below = row_of(r + 1)
                    halves.append(
                        jnp.concatenate(
                            [toeplitz(below[part], above[part]) for part in range(2)], axis=1
                        )
                    )
                    above = below
                right = jnp.concatenate(halves, axis=0)
                s0 = surv[2 * quad]
                s1 = surv[2 * quad + 1]
                left = jnp.concatenate(
                    [
                        jnp.concatenate([jnp.where(low, s0, nil), nil], axis=1),
                        jnp.concatenate([jnp.where(low, nil, s0), nil], axis=1),
                        jnp.concatenate([nil, jnp.where(low, s1, nil)], axis=1),
                        jnp.concatenate([nil, jnp.where(low, nil, s1)], axis=1),
                    ],
                    axis=0,
                )
                prod = jnp.dot(left, right, preferred_element_type=F32)
                for l in range(4):
                    re = prod[32 * l : 32 * l + 16]
                    im = prod[32 * l + 16 : 32 * l + 32]
                    cre = re[:, :LANES] + im[:, LANES:]
                    cim = im[:, :LANES] - re[:, LANES:]
                    for half in range(2):
                        at = pl.multiple_of((2 * quad + l // 2) * 8, 8) + (l % 2) * 4 * BLOCKS
                        at = at + half * 8 * BLOCKS
                        corr_re[pl.ds(at, 8), :] = cre[8 * half : 8 * half + 8]
                        corr_im[pl.ds(at, 8), :] = cim[8 * half : 8 * half + 8]
            return 0

        lax.fori_loop(0, WINDOWS // (2 * QUADS), pair, 0)

        for c in range(4):
            piece = roots[pl.ds(4 * doppler[k] + c, DOPPLER, stride=4), :].astype(BF16)
            table[:DOPPLER, c * LANES : (c + 1) * LANES] = piece
            if c < 2:
                table[DOPPLER:, BLOCKS + c * LANES : BLOCKS + (c + 1) * LANES] = piece
            else:
                table[DOPPLER:, (c - 2) * LANES : (c - 1) * LANES] = -piece

        def beams(step, _):
            half = 1 - step

            def column(ref, b):
                at = half * 8 * BLOCKS + b
                even = ref[pl.ds(at, LANES, stride=8), :].astype(BF16)
                odd = ref[pl.ds(at + 8 * LANES, LANES, stride=8), :].astype(BF16)
                return jnp.concatenate([even, pltpu.roll(odd, BLOCK_LEN, axis=1)], axis=0)

            for bp in range(4):
                right = jnp.concatenate(
                    [
                        jnp.concatenate([column(ref, 2 * bp), column(ref, 2 * bp + 1)], axis=1)
                        for ref in (corr_re, corr_im)
                    ],
                    axis=0,
                )
                spec = jnp.dot(table[...], right, preferred_element_type=F32)
                sre, sim = spec[:DOPPLER], spec[DOPPLER:]
                power = (sre * sre + sim * sim) * (1.0 / (4 * BLOCKS * BLOCK_LEN))
                for b in range(2):
                    turned = power[:, b * LANES : (b + 1) * LANES].T.astype(BF16)
                    for g in range(SEG):
                        outbox[k, half, g // 2, g % 2, 2 * bp + b] = turned[16 * g : 16 * (g + 1)]
            first(k, half)
            return 0

        lax.fori_loop(0, 2, beams, 0)

        @pl.when(k == 0)
        def _():
            arrive(1)

        @pl.when(k > 0)
        def _():
            second(k - 1)

        return 0

    lax.fori_loop(0, TX, transmitter, 0)

    for g in range(2):
        for o in range(1, BEAM):
            scatter(g, o).wait_send()
            spread(g, o).wait_send()

    def collect(k, _):
        total = sum_x[k, my_z].astype(F32)
        for dz in range(1, 4):
            around_last(k, dz).wait_recv()
            total = total + last_z[k, dz].astype(F32)
        out[k, 0:8] = total * (1.0 / SEG)
        across_last(k).wait_recv()
        total = sum_z[k, my_x].astype(F32) + last_x[k].astype(F32)
        out[k, 8:16] = total * (1.0 / SEG)
        across(k).wait_send()
        across_last(k).wait_send()
        for dz in range(1, 4):
            around(k, dz).wait_send()
            around_last(k, dz).wait_send()
        return 0

    lax.fori_loop(0, TX - 1, collect, 0)

    for half in range(2):
        total = outbox[TX - 1, half, my_z, my_x].astype(F32)
        for o in range(1, SEG):
            straight(half, o).wait_recv()
            total = total + inbox[half, o].astype(F32)
        out[TX - 1, 8 * half : 8 * half + 8] = total * (1.0 / SEG)
    for half in range(2):
        for o in range(1, SEG):
            straight(half, o).wait_send()


def root_table():
    ells = np.arange(BLOCKS).reshape(LANES, 2).T.reshape(1, BLOCKS)
    freqs = np.arange(2 * DOPPLER)[:, None] - BLOCKS // 2
    angle = 2.0 * np.pi / BLOCKS * ((ells * freqs) % BLOCKS)
    both = np.concatenate([np.cos(angle), np.sin(angle)], axis=1)
    return jnp.asarray(both.reshape(8 * DOPPLER, LANES), F32)


def shards(voltages, surv_taps, ref_taps, tx_owner, delay_start, doppler_start):
    smem = pl.BlockSpec(memory_space=pltpu.SMEM)
    hbm = pl.BlockSpec(memory_space=pl.ANY)
    dma = pltpu.SemaphoreType.DMA
    raw = DECIM * WINDOWS * LANES
    return pl.pallas_call(
        main_kernel,
        in_specs=[smem] * 5 + [hbm] * 2,
        out_specs=pl.BlockSpec(memory_space=pltpu.VMEM),
        out_shape=jax.ShapeDtypeStruct((TX, BEAMS_HERE, DELAYS // SEG, DOPPLER), F32),
        scratch_shapes=[
            pltpu.VMEM((2, BEAMS_HERE, raw + LANES), BF16),
            pltpu.VMEM((8 * DOPPLER, LANES), F32),
            pltpu.VMEM((5 * LANES, 2 * LANES), BF16),
            pltpu.VMEM((WINDOWS, 32, LANES), BF16),
            pltpu.VMEM((4 * REGION, LANES), F32),
            pltpu.VMEM((TX, BEAM, 16, LANES), BF16),
            pltpu.VMEM((BEAM, TX, 16, LANES), BF16),
            pltpu.VMEM((TX, 16, LANES), BF16),
            pltpu.VMEM((TX, BEAM, 16, LANES), BF16),
            pltpu.VMEM((2 * TX, WINDOWS, LANES), F32),
            pltpu.VMEM((2 * TX, WINDOWS + 1, 16, LANES), BF16),
            pltpu.VMEM((BEAMS_HERE * BLOCKS, LANES), F32),
            pltpu.VMEM((BEAMS_HERE * BLOCKS, LANES), F32),
            pltpu.VMEM((2 * DOPPLER, 2 * BLOCKS), BF16),
            pltpu.VMEM((TX, 2, 4, 2, 8, 16, LANES), BF16),
            pltpu.VMEM((TX, 4, 8, 16, LANES), BF16),
            pltpu.VMEM((TX, 4, 2, 8, 16, LANES), BF16),
            pltpu.VMEM((TX, 4, 8, 16, LANES), BF16),
            pltpu.VMEM((TX, 2, 8, 16, LANES), BF16),
            pltpu.VMEM((TX, 8, 16, LANES), BF16),
            pltpu.VMEM((TX, 4, 8, 16, LANES), BF16),
            pltpu.VMEM((2, SEG, 8, 16, LANES), BF16),
            dma((STEPS,)),
            dma,
            dma((2, BEAM)),
            dma((2, BEAM)),
            dma((2, BEAM)),
            dma((2, BEAM)),
            dma((TX, 4)),
            dma((TX, 4)),
            dma((TX, 4)),
            dma((TX, 4)),
            dma((2, SEG)),
            dma((2, SEG)),
        ],
        compiler_params=pltpu.CompilerParams(collective_id=0, has_side_effects=True),
        name="ambiguity",
    )(
        tx_owner,
        delay_start,
        doppler_start,
        surv_taps,
        ref_taps,
        voltages.reshape(2, BEAMS_HERE, raw),
        root_table(),
    )


def solution(mesh):
    return jax.shard_map(
        shards,
        mesh=mesh,
        in_specs=(P(None, "beam", "seg", None), P(), P(), P(), P(), P()),
        out_specs=P(None, "beam", "seg", None),
        check_vma=False,
    )
```

```python
import functools

import jax
import jax.numpy as jnp
import numpy as np
from jax import lax
from jax.experimental import pallas as pl
from jax.experimental.pallas import tpu as pltpu
from jax.sharding import PartitionSpec as P

TX = 4
DECIM = 4
TAPS = 32
BLOCK_LEN = 64
BLOCKS = 256
DELAYS = 128
DOPPLER = 128
LANES = 128
BEAMS_HERE = 16
WINDOWS = 128
WINDOWS_STEP = 32
CHUNK = WINDOWS_STEP * 512
STEPS = WINDOWS // WINDOWS_STEP
RAW_WINDOW = DECIM * LANES
REGION = (WINDOWS + 8) * 8
BEAM = 16
SEG = 8
QUADS = 64
F32 = jnp.float32
BF16 = jnp.bfloat16
MESH = pl.DeviceIdType.MESH


def band_base(taps, backwards):
    rows = lax.broadcasted_iota(jnp.int32, (LANES, LANES), 0)
    cols = lax.broadcasted_iota(jnp.int32, (LANES, LANES), 1)
    if backwards:
        cols = LANES - 1 - cols
    offset = DECIM * cols - rows
    total = jnp.zeros((LANES, LANES), F32)
    for tap in range(TAPS):
        total = jnp.where(offset == tap, taps[tap].astype(F32), total)
    return total


def main_kernel(
    owner,
    delay,
    doppler,
    surv_taps,
    ref_taps,
    x_hbm,
    roots_hbm,
    out,
    x,
    roots,
    band,
    surv,
    picked,
    ref_in,
    gathered,
    reduced,
    refs,
    rows,
    leaning,
    corr_re,
    corr_im,
    table,
    outbox,
    in_x,
    in_z,
    sum_x,
    sum_z,
    last_x,
    last_z,
    inbox,
    sem_x,
    sem_roots,
    send_a,
    recv_a,
    send_b,
    recv_b,
    send_c,
    recv_c,
    send_d,
    recv_d,
    send_e,
    recv_e,
):
    my_beam = lax.axis_index("beam")
    my_seg = lax.axis_index("seg")

    def fetch(c):
        at = pl.multiple_of(c * CHUNK, LANES)
        return pltpu.make_async_copy(
            x_hbm.at[:, :, pl.ds(at, CHUNK)],
            x.at[:, :, pl.ds(at + LANES, CHUNK)],
            sem_x.at[c],
        )

    for c in range(STEPS):
        fetch(c).start()
    fetch_roots = pltpu.make_async_copy(roots_hbm, roots, sem_roots)
    fetch_roots.start()

    barrier = pltpu.get_barrier_semaphore()
    for o in range(1, BEAM):
        peer = lax.rem(my_beam + o, BEAM)
        pl.semaphore_signal(barrier, inc=1, device_id={"beam": peer}, device_id_type=MESH)
    for o in range(1, SEG):
        peer = lax.rem(my_seg + o, SEG)
        pl.semaphore_signal(barrier, inc=1, device_id={"seg": peer}, device_id_type=MESH)

    wide = lax.broadcasted_iota(jnp.int32, (LANES, LANES), 1)
    forward = band_base(surv_taps, False)
    backward = band_base(ref_taps, True)
    for part in range(5):
        shift = 32 * (part - 1)
        ahead = pltpu.roll(forward, shift % LANES, axis=1)
        behind = pltpu.roll(backward, -shift % LANES, axis=1)
        if part == 0:
            ahead = jnp.where(wide < 8, ahead, 0.0)
            behind = jnp.where(wide >= LANES - 8, behind, 0.0)
        else:
            ahead = jnp.where(wide >= shift, ahead, 0.0)
            behind = jnp.where(wide < LANES - shift, behind, 0.0)
        band[part * LANES : (part + 1) * LANES, :LANES] = ahead.astype(BF16)
        band[part * LANES : (part + 1) * LANES, LANES:] = behind.astype(BF16)
    x[:, :, :LANES] = jnp.zeros((2, BEAMS_HERE, LANES), BF16)
    for r in range(4):
        picked[r * REGION + WINDOWS * 8 : (r + 1) * REGION, :] = jnp.zeros((64, LANES), F32)

    def decimate(step, _):
        fetch(step).wait()
        for group in range(WINDOWS_STEP // 8):
            pieces = []
            for w in range(8):
                q = step * WINDOWS_STEP + group * 8 + w
                at = pl.multiple_of(q * RAW_WINDOW, LANES)
                for part in range(2):
                    pieces.append(x[part, :, pl.ds(at, RAW_WINDOW + LANES)])
            left = jnp.concatenate(pieces, axis=0)
            both = jnp.dot(left, band[...], preferred_element_type=F32)
            for w in range(8):
                q = step * WINDOWS_STEP + group * 8 + w
                part_rows = both[w * 32 : (w + 1) * 32]
                surv[q] = part_rows[:, :LANES].astype(BF16)
                at = pl.multiple_of((WINDOWS - 1 - q) * 8, 8)
                for r in range(4):
                    picked[pl.ds(at + r * REGION, 8), :] = part_rows[8 * r : 8 * r + 8, LANES:]
        return 0

    lax.fori_loop(0, STEPS, decimate, 0)

    def pick(k):
        mine = lax.div(owner[k], BEAMS_HERE) == my_beam
        local = lax.rem(owner[k], BEAMS_HERE)
        whole = lax.div(delay[k], LANES)
        rest = lax.rem(delay[k], LANES)
        turn = lax.rem(LANES - rest, LANES)
        for part in range(2):
            start = (2 * part + lax.div(local, 8)) * REGION + whole * 8 + lax.rem(local, 8)
            first = picked[pl.ds(start, WINDOWS, stride=8), :]
            second = picked[pl.ds(start + 8, WINDOWS, stride=8), :]
            moved = jnp.where(
                wide < LANES - rest,
                pltpu.roll(first, turn, axis=1),
                pltpu.roll(second, turn, axis=1),
            )
            moved = jnp.where(mine, moved, 0.0).astype(BF16)
            ref_in[k, part * 8 : (part + 1) * 8] = moved.reshape(8, 16, LANES)

    groups = ((0, 1), (1, 1), (2, 2))

    def scatter(g, o):
        base, count = groups[g]
        peer = lax.rem(my_beam + o, BEAM)
        return pltpu.make_async_remote_copy(
            src_ref=ref_in.at[pl.ds(base, count), peer],
            dst_ref=gathered.at[o, pl.ds(base, count)],
            send_sem=send_a.at[g, o],
            recv_sem=recv_a.at[g, o],
            device_id={"beam": peer},
            device_id_type=MESH,
        )

    def spread(g, o):
        base, count = groups[g]
        peer = lax.rem(my_beam + o, BEAM)
        return pltpu.make_async_remote_copy(
            src_ref=reduced.at[pl.ds(base, count)],
            dst_ref=refs.at[pl.ds(base, count), my_beam],
            send_sem=send_b.at[g, o],
            recv_sem=recv_b.at[g, o],
            device_id={"beam": peer},
            device_id_type=MESH,
        )

    def spread_sums(g):
        base, count = groups[g]
        total = ref_in[base : base + count, my_beam].astype(F32)
        for o in range(1, BEAM):
            scatter(g, o).wait_recv()
            total = total + gathered[o, base : base + count].astype(F32)
        reduced[base : base + count] = total.astype(BF16)
        for o in range(1, BEAM):
            spread(g, o).start()
        refs[base : base + count, my_beam] = reduced[base : base + count]

    def arrive(g):
        base, count = groups[g]
        for o in range(1, BEAM):
            spread(g, o).wait_recv()
        for k in range(base, base + count):
            for part in range(2):
                flat = refs[k, part * 8 : (part + 1) * 8].reshape(WINDOWS, LANES)
                rows[2 * k + part, :WINDOWS] = flat.astype(F32)

        def stagger(step, _):
            for r in range(64):
                kp = 2 * base + lax.div(step, 2)
                i = lax.rem(step, 2) * 64 + r
                row = jnp.broadcast_to(rows[kp, pl.ds(i, 1), :], (8, LANES))
                top = pltpu.roll(row, 1, axis=1, stride=1, stride_axis=0)
                bottom = pltpu.roll(row, 9, axis=1, stride=1, stride_axis=0)
                leaning[kp, i] = jnp.concatenate([top, bottom], axis=0).astype(BF16)
            return 0

        lax.fori_loop(0, 4 * count, stagger, 0)

    pick(0)
    pl.semaphore_wait(barrier, BEAM - 1 + SEG - 1)
    for o in range(1, BEAM):
        scatter(0, o).start()
    pick(1)
    for o in range(1, BEAM):
        scatter(1, o).start()
    for k in range(2, TX):
        pick(k)
    for o in range(1, BEAM):
        scatter(2, o).start()
    fetch_roots.wait()
    spread_sums(0)
    spread_sums(1)
    spread_sums(2)
    arrive(0)

    lane = lax.broadcasted_iota(jnp.int32, (16, LANES), 1)
    sub = lax.broadcasted_iota(jnp.int32, (16, LANES), 0)
    low = lax.broadcasted_iota(jnp.int32, (32, LANES), 1) < BLOCK_LEN
    nil = jnp.zeros((32, LANES), BF16)

    my_z = lax.div(my_seg, 2)
    my_x = lax.rem(my_seg, 2)
    other = {"seg": 2 * my_z + 1 - my_x}

    def ring(dz):
        z = lax.rem(my_z + dz, 4)
        return z, {"seg": 2 * z + my_x}

    def remote(src, dst, send, recv, device):
        return pltpu.make_async_remote_copy(
            src_ref=src,
            dst_ref=dst,
            send_sem=send,
            recv_sem=recv,
            device_id=device,
            device_id_type=MESH,
        )

    def across(k):
        return remote(
            outbox.at[k, 0, :, 1 - my_x], in_x.at[k], send_c.at[k, 0], recv_c.at[k, 0], other
        )

    def around(k, dz):
        z, device = ring(dz)
        return remote(
            outbox.at[k, 1, z], in_z.at[k, dz], send_c.at[k, dz], recv_c.at[k, dz], device
        )

    def across_last(k):
        return remote(
            sum_z.at[k, 1 - my_x], last_x.at[k], send_d.at[k, 0], recv_d.at[k, 0], other
        )

    def around_last(k, dz):
        z, device = ring(dz)
        return remote(
            sum_x.at[k, z], last_z.at[k, dz], send_d.at[k, dz], recv_d.at[k, dz], device
        )

    def second(k):
        for dz in range(1, 4):
            around(k, dz).wait_recv()
        for side in range(2):
            total = outbox[k, 1, my_z, side].astype(F32)
            for dz in range(1, 4):
                total = total + in_z[k, dz, side].astype(F32)
            sum_z[k, side] = total.astype(BF16)
        across_last(k).start()
        across(k).wait_recv()
        for z in range(4):
            total = outbox[k, 0, z, my_x].astype(F32) + in_x[k, z].astype(F32)
            sum_x[k, z] = total.astype(BF16)
        for dz in range(1, 4):
            around_last(k, dz).start()

    def straight(half, o):
        peer = lax.rem(my_seg + o, SEG)
        return remote(
            outbox.at[TX - 1, half, lax.div(peer, 2), lax.rem(peer, 2)],
            inbox.at[half, o],
            send_e.at[half, o],
            recv_e.at[half, o],
            {"seg": peer},
        )

    def first(k, half):
        @pl.when((half == 0) & (k < TX - 1))
        def _():
            across(k).start()

        @pl.when((half == 1) & (k < TX - 1))
        def _():
            for dz in range(1, 4):
                around(k, dz).start()

        @pl.when(k == TX - 1)
        def _():
            for o in range(1, SEG):
                straight(half, o).start()

    for kp in range(2 * TX):
        leaning[kp, WINDOWS] = jnp.zeros((16, LANES), BF16)

    def staggered(kp, i):
        return leaning[kp, i]

    def turns(u):
        return [u] + [pltpu.roll(u, 16 * c, axis=1) for c in range(1, 4)]

    def toeplitz(below, above):
        even, odd = [], []
        for c in range(4):
            near = lane < sub + 1 + 16 * c
            even.append(jnp.where(near, below[c], above[c]))
            odd.append(jnp.where(near | (lane >= BLOCK_LEN), below[c], above[c]))
        return jnp.concatenate(even + odd, axis=0)

    def transmitter(k, _):
        def pair(step, _):
            def row_of(r):
                return [turns(staggered(2 * k + part, WINDOWS - 2 * QUADS * step - r)) for part in range(2)]

            above = row_of(0)
            for sub_q in range(QUADS):
                quad = QUADS * step + sub_q
                halves = []
                for a in range(2):
                    r = 2 * sub_q + a
                    below = row_of(r + 1)
                    halves.append(
                        jnp.concatenate(
                            [toeplitz(below[part], above[part]) for part in range(2)], axis=1
                        )
                    )
                    above = below
                right = jnp.concatenate(halves, axis=0)
                s0 = surv[2 * quad]
                s1 = surv[2 * quad + 1]
                left = jnp.concatenate(
                    [
                        jnp.concatenate([jnp.where(low, s0, nil), nil], axis=1),
                        jnp.concatenate([jnp.where(low, nil, s0), nil], axis=1),
                        jnp.concatenate([nil, jnp.where(low, s1, nil)], axis=1),
                        jnp.concatenate([nil, jnp.where(low, nil, s1)], axis=1),
                    ],
                    axis=0,
                )
                prod = jnp.dot(left, right, preferred_element_type=F32)
                for l in range(4):
                    re = prod[32 * l : 32 * l + 16]
                    im = prod[32 * l + 16 : 32 * l + 32]
                    cre = re[:, :LANES] + im[:, LANES:]
                    cim = im[:, :LANES] - re[:, LANES:]
                    for half in range(2):
                        at = pl.multiple_of((2 * quad + l // 2) * 8, 8) + (l % 2) * 4 * BLOCKS
                        at = at + half * 8 * BLOCKS
                        corr_re[pl.ds(at, 8), :] = cre[8 * half : 8 * half + 8]
                        corr_im[pl.ds(at, 8), :] = cim[8 * half : 8 * half + 8]
            return 0

        lax.fori_loop(0, WINDOWS // (2 * QUADS), pair, 0)

        for c in range(4):
            piece = roots[pl.ds(4 * doppler[k] + c, DOPPLER, stride=4), :].astype(BF16)
            table[:DOPPLER, c * LANES : (c + 1) * LANES] = piece
            if c < 2:
                table[DOPPLER:, BLOCKS + c * LANES : BLOCKS + (c + 1) * LANES] = piece
            else:
                table[DOPPLER:, (c - 2) * LANES : (c - 1) * LANES] = -piece

        def beams(step, _):
            half = 1 - step

            def column(ref, b):
                at = half * 8 * BLOCKS + b
                even = ref[pl.ds(at, LANES, stride=8), :].astype(BF16)
                odd = ref[pl.ds(at + 8 * LANES, LANES, stride=8), :].astype(BF16)
                return jnp.concatenate([even, pltpu.roll(odd, BLOCK_LEN, axis=1)], axis=0)

            for bp in range(4):
                right = jnp.concatenate(
                    [
                        jnp.concatenate([column(ref, 2 * bp), column(ref, 2 * bp + 1)], axis=1)
                        for ref in (corr_re, corr_im)
                    ],
                    axis=0,
                )
                spec = jnp.dot(table[...], right, preferred_element_type=F32)
                sre, sim = spec[:DOPPLER], spec[DOPPLER:]
                power = (sre * sre + sim * sim) * (1.0 / (4 * BLOCKS * BLOCK_LEN))
                for b in range(2):
                    turned = power[:, b * LANES : (b + 1) * LANES].T.astype(BF16)
                    for g in range(SEG):
                        outbox[k, half, g // 2, g % 2, 2 * bp + b] = turned[16 * g : 16 * (g + 1)]
            first(k, half)
            return 0

        lax.fori_loop(0, 2, beams, 0)

        @pl.when(k == 0)
        def _():
            arrive(1)

        @pl.when(k == 1)
        def _():
            arrive(2)

        @pl.when(k > 0)
        def _():
            second(k - 1)

        return 0

    lax.fori_loop(0, TX, transmitter, 0)

    for g in range(3):
        for o in range(1, BEAM):
            scatter(g, o).wait_send()
            spread(g, o).wait_send()

    def collect(k, _):
        total = sum_x[k, my_z].astype(F32)
        for dz in range(1, 4):
            around_last(k, dz).wait_recv()
            total = total + last_z[k, dz].astype(F32)
        out[k, 0:8] = total * (1.0 / SEG)
        across_last(k).wait_recv()
        total = sum_z[k, my_x].astype(F32) + last_x[k].astype(F32)
        out[k, 8:16] = total * (1.0 / SEG)
        across(k).wait_send()
        across_last(k).wait_send()
        for dz in range(1, 4):
            around(k, dz).wait_send()
            around_last(k, dz).wait_send()
        return 0

    lax.fori_loop(0, TX - 1, collect, 0)

    for half in range(2):
        total = outbox[TX - 1, half, my_z, my_x].astype(F32)
        for o in range(1, SEG):
            straight(half, o).wait_recv()
            total = total + inbox[half, o].astype(F32)
        out[TX - 1, 8 * half : 8 * half + 8] = total * (1.0 / SEG)
    for half in range(2):
        for o in range(1, SEG):
            straight(half, o).wait_send()


def root_table():
    ells = np.arange(BLOCKS).reshape(LANES, 2).T.reshape(1, BLOCKS)
    freqs = np.arange(2 * DOPPLER)[:, None] - BLOCKS // 2
    angle = 2.0 * np.pi / BLOCKS * ((ells * freqs) % BLOCKS)
    both = np.concatenate([np.cos(angle), np.sin(angle)], axis=1)
    return jnp.asarray(both.reshape(8 * DOPPLER, LANES), F32)


def shards(voltages, surv_taps, ref_taps, tx_owner, delay_start, doppler_start):
    smem = pl.BlockSpec(memory_space=pltpu.SMEM)
    hbm = pl.BlockSpec(memory_space=pl.ANY)
    dma = pltpu.SemaphoreType.DMA
    raw = DECIM * WINDOWS * LANES
    return pl.pallas_call(
        main_kernel,
        in_specs=[smem] * 5 + [hbm] * 2,
        out_specs=pl.BlockSpec(memory_space=pltpu.VMEM),
        out_shape=jax.ShapeDtypeStruct((TX, BEAMS_HERE, DELAYS // SEG, DOPPLER), F32),
        scratch_shapes=[
            pltpu.VMEM((2, BEAMS_HERE, raw + LANES), BF16),
            pltpu.VMEM((8 * DOPPLER, LANES), F32),
            pltpu.VMEM((5 * LANES, 2 * LANES), BF16),
            pltpu.VMEM((WINDOWS, 32, LANES), BF16),
            pltpu.VMEM((4 * REGION, LANES), F32),
            pltpu.VMEM((TX, BEAM, 16, LANES), BF16),
            pltpu.VMEM((BEAM, TX, 16, LANES), BF16),
            pltpu.VMEM((TX, 16, LANES), BF16),
            pltpu.VMEM((TX, BEAM, 16, LANES), BF16),
            pltpu.VMEM((2 * TX, WINDOWS, LANES), F32),
            pltpu.VMEM((2 * TX, WINDOWS + 1, 16, LANES), BF16),
            pltpu.VMEM((BEAMS_HERE * BLOCKS, LANES), F32),
            pltpu.VMEM((BEAMS_HERE * BLOCKS, LANES), F32),
            pltpu.VMEM((2 * DOPPLER, 2 * BLOCKS), BF16),
            pltpu.VMEM((TX, 2, 4, 2, 8, 16, LANES), BF16),
            pltpu.VMEM((TX, 4, 8, 16, LANES), BF16),
            pltpu.VMEM((TX, 4, 2, 8, 16, LANES), BF16),
            pltpu.VMEM((TX, 4, 8, 16, LANES), BF16),
            pltpu.VMEM((TX, 2, 8, 16, LANES), BF16),
            pltpu.VMEM((TX, 8, 16, LANES), BF16),
            pltpu.VMEM((TX, 4, 8, 16, LANES), BF16),
            pltpu.VMEM((2, SEG, 8, 16, LANES), BF16),
            dma((STEPS,)),
            dma,
            dma((3, BEAM)),
            dma((3, BEAM)),
            dma((3, BEAM)),
            dma((3, BEAM)),
            dma((TX, 4)),
            dma((TX, 4)),
            dma((TX, 4)),
            dma((TX, 4)),
            dma((2, SEG)),
            dma((2, SEG)),
        ],
        compiler_params=pltpu.CompilerParams(collective_id=0, has_side_effects=True),
        name="ambiguity",
    )(
        tx_owner,
        delay_start,
        doppler_start,
        surv_taps,
        ref_taps,
        voltages.reshape(2, BEAMS_HERE, raw),
        root_table(),
    )


def solution(mesh):
    return jax.shard_map(
        shards,
        mesh=mesh,
        in_specs=(P(None, "beam", "seg", None), P(), P(), P(), P(), P()),
        out_specs=P(None, "beam", "seg", None),
        check_vma=False,
    )
```
